512 devices in a mesh: dp: 8 (over z), expert: 64 (over y, x, core).
Axes of the slice: x: 4, y: 8, z: 8, core: 2. Of those that a mesh axis runs over, the one named last changes fastest.
Arguments:
- inputs: bfloat16 [8, 64, 256, 256], P('dp', 'expert'), may hold values from -6 to 6
- layer_weights: bfloat16 [64, 8, 256, 256], P('expert'), may hold values from -0.375 to 0.375
- layer_biases: float32 [64, 8, 256], P('expert'), may hold values from -3 to 3
- head_weight: bfloat16 [4, 256], replicated, may hold values from -0.375 to 0.375
- head_bias: float32 [4], replicated, may hold values from -3 to 3
- gate_values: float32 [8, 64, 256], P('dp', 'expert'), may hold values from 0.3 to 1
- spacing: float32 [8, 64, 256], P('dp', 'expert'), may hold values from 0.004 to 0.04
- ray_index: int32 [8, 64, 256], P('dp', 'expert'), may hold values from 0 to 3, never falling along the last dimension, each value on 1 to 96 neighbouring positions
- expert_index: int32 [8, 64, 256], P('dp', 'expert'), may hold values from 0 to 63, as said below
- slot_index: int32 [8, 64, 256], P('dp', 'expert'), may hold values from 0 to 7, as said below
- color_cotangent: float32 [8, 64, 3, 4], P('dp', 'expert'), may hold values from -6 to 6
Outputs:
- grad_inputs: bfloat16 [8, 64, 256, 256], P('dp', 'expert')
- grad_weights: float32 [64, 8, 256, 256], P('expert')
- grad_biases: float32 [64, 8, 256], P('expert')
- grad_head_weight: float32 [4, 256], replicated
- grad_head_bias: float32 [4], replicated
The draws below stay inside these ranges and needn't reach their ends.
Inputs may be any that keep to these rules, and one draw needn't show every extreme that they name: `expert_index`: on each device, at most 8 samples name one expert; one expert, the same on every device, is named by exactly 8 samples on every device. `slot_index`: on each device, the n samples that name one expert hold the slots 0 to n - 1, each once. `ray_index`: never falling along the samples of a device; every ray 0 to 3 holds 1 to 96 consecutive samples, and some ray exactly 96.
All inputs are finite; a program needn't handle non-finite values.
Results may differ from the reference program's by a relative error of at most 0.02.
Values may be sent and summed in bfloat16 or wider, within the bound.
A program may use at most 64 MiB of HBM per device.

```python
import math
import jax
import jax.numpy as jnp
import numpy as np
from jax import lax

D = 256
LAYERS = 8
HEAD = 4
RAYS_DEV = 4
REPLICAS = 8
EXPERTS = 64
SAMPLES_DEV = 256
CAP = 8
RAY_MOST = 96


def routing_tables(key):
    base = jax.random.fold_in(key, 913)
    full_expert = jax.random.randint(jax.random.fold_in(base, 1), (), 0, EXPERTS)

    def one_device(device_key):
        subkeys = jax.random.split(device_key, 3)
        hotness = jax.random.randint(subkeys[0], (EXPERTS,), 0, 4 * CAP)
        hotness = jnp.where(jnp.arange(EXPERTS) == full_expert, 8 * CAP, hotness)
        levels = hotness[:, None] - 4 * jnp.arange(CAP)[None, :]
        breakers = jax.random.permutation(subkeys[1], EXPERTS * CAP)
        scores = levels.reshape(-1) * (EXPERTS * CAP) + breakers
        _, chosen = lax.top_k(scores, SAMPLES_DEV)
        shuffled = chosen[jax.random.permutation(subkeys[2], SAMPLES_DEV)]
        return (shuffled // CAP, shuffled % CAP)
    device_keys = jax.vmap(lambda number: jax.random.fold_in(base, number + 7))(jnp.arange(REPLICAS * EXPERTS))
    experts_drawn, slots_drawn = jax.vmap(one_device)(device_keys)
    experts_drawn = experts_drawn.reshape(REPLICAS, EXPERTS, SAMPLES_DEV).astype(jnp.int32)
    slots_drawn = slots_drawn.reshape(REPLICAS, EXPERTS, SAMPLES_DEV).astype(jnp.int32)
    return (experts_drawn, slots_drawn)


def draw_expert_index(key, part):
    return routing_tables(key)[0]


def draw_slot_index(key, part):
    return routing_tables(key)[1]


def block_scale(key, extent, cuts, smallest, top_value):
    def one(position, blocks):
        draws = jax.random.uniform(jax.random.fold_in(jax.random.fold_in(key, 6), position), (blocks,), jnp.float32, smallest / len(cuts), top_value / len(cuts))
        return jnp.repeat(jnp.exp(draws), extent[position] // blocks).reshape((-1,) + (1,) * (len(extent) - position - 1))

    factor_of = one(*cuts[0])
    for cut in cuts[1:]:
        factor_of = factor_of * one(*cut)
    return factor_of


def profile(count, total, most, lean):
    portions = [(1 << 20) // math.isqrt(standing ** lean) + 1 for standing in range(2, count + 1)]
    surplus, given = total - most - (count - 1), [1] * (count - 1)
    while surplus > 0:
        movable = [i for i in range(count - 1) if given[i] < most]
        pool, remaining = sum([portions[i] for i in movable]), surplus
        for i in movable:
            extra = min(most - given[i], max(1, remaining * portions[i] // pool), surplus)
            given[i] = given[i] + extra
            surplus = surplus - extra
    return np.array([most] + given)


def ragged_sizes(key, count, total, limit, skew):
    if count == 2:
        one = jax.random.randint(key, (), max(1, total - limit), min(limit, total - 1) + 1)
        return jnp.stack([one, total - one])
    tallies = jnp.asarray(profile(count, total, limit, skew), jnp.int32)
    twos = (count - 1) // 2
    source_of, receiver = tallies[1:1 + 2 * twos:2], tallies[2:2 + 2 * twos:2]
    margin = jnp.minimum(source_of - 1, limit - receiver)
    shifted = jax.random.randint(jax.random.fold_in(key, 1), (twos,), 0, 1 << 20) % (margin + 1)
    tallies = tallies.at[1:1 + 2 * twos:2].set(source_of - shifted).at[2:2 + 2 * twos:2].set(receiver + shifted)
    return tallies[jax.random.permutation(jax.random.fold_in(key, 2), count)]


def normal_values(key, shape, deviation, bound, shards=(), kind=jnp.bfloat16):
    values = jax.random.normal(key, shape, jnp.float32) * deviation
    if len(shards) > 0:
        values = block_scale(key, shape, shards, -0.22, 0.18) * values
    return jnp.clip(values, min=-bound, max=bound).astype(kind)


def setup_inputs(seed: int = 0) -> dict:
    keys = jax.random.split(jax.random.key(seed), 12)
    return {
        "inputs": normal_values(keys[0], (REPLICAS, EXPERTS, SAMPLES_DEV, D), 1.0, 6.0, ((0, 8), (1, 64))),
        "layer_weights": normal_values(keys[1], (EXPERTS, LAYERS, D, D), D ** -0.5, 0.375, ((0, 64),)),
        "layer_biases": normal_values(keys[2], (EXPERTS, LAYERS, D), 0.5, 3.0, ((0, 64),), jnp.float32),
        "head_weight": normal_values(keys[3], (HEAD, D), D ** -0.5, 0.375),
        "head_bias": normal_values(keys[4], (HEAD,), 1.0, 3.0, (), jnp.float32),
        "gate_values": jnp.clip(0.3 + 0.7 * jax.random.uniform(keys[5], (REPLICAS, EXPERTS, SAMPLES_DEV), jnp.float32) ** block_scale(keys[5], (REPLICAS, EXPERTS, SAMPLES_DEV), ((0, 8), (1, 64)), -0.2, 0.2), 0.3, 1.0),
        "spacing": jnp.clip(jnp.exp(math.log(0.04) - 2.30258502 * jax.random.uniform(keys[6], (REPLICAS, EXPERTS, SAMPLES_DEV), jnp.float32) ** block_scale(keys[6], (REPLICAS, EXPERTS, SAMPLES_DEV), ((0, 8), (1, 64)), -0.2, 0.2)), 0.004, 0.04),
        "ray_index": jax.vmap(lambda own: jnp.searchsorted(jnp.cumsum(ragged_sizes(own, RAYS_DEV, SAMPLES_DEV, RAY_MOST, 2)), jnp.arange(SAMPLES_DEV), side="right"))(jax.random.split(keys[7], REPLICAS * EXPERTS)).reshape((REPLICAS, EXPERTS, SAMPLES_DEV)).astype(jnp.int32),
        "expert_index": draw_expert_index(jax.random.fold_in(keys[11], 71), 0),
        "slot_index": draw_slot_index(jax.random.fold_in(keys[11], 71), 0),
        "color_cotangent": normal_values(keys[10], (REPLICAS, EXPERTS, 3, RAYS_DEV), 1.0, 6.0, ((0, 8), (1, 64)), jnp.float32),
    }


def forward(rows, weights, biases):
    activations = [rows]
    current = rows
    outcome = None
    for number in range(LAYERS):
        summed = jnp.dot(current, weights[number], preferred_element_type=jnp.float32) + biases[number]
        if number < LAYERS - 1:
            current = jax.nn.softplus(summed).astype(jnp.bfloat16)
            activations.append(current)
        else:
            outcome = summed.astype(jnp.bfloat16)
    return (activations, outcome)

def backward(activations, weights, upstream):
    weight_grads = [None] * LAYERS
    bias_grads = [None] * LAYERS
    input_rows = None
    for number in reversed(range(LAYERS)):
        weight_grads[number] = lax.dot_general(activations[number], upstream, (((0,), (0,)), ((), ())), preferred_element_type=jnp.float32)
        bias_grads[number] = lax.optimization_barrier(jnp.sum(upstream.astype(jnp.float32), axis=0))
        spread = lax.dot_general(upstream, weights[number], (((1,), (1,)), ((), ())), preferred_element_type=jnp.float32)
        if number > 0:
            slope = -jnp.expm1(-activations[number].astype(jnp.float32))
            upstream = (spread * slope).astype(jnp.bfloat16)
        else:
            input_rows = spread.astype(jnp.bfloat16)
    return (jnp.stack(weight_grads), jnp.stack(bias_grads), input_rows)

def head_product(features, head_weight):
    return lax.dot_general(features, head_weight, (((1,), (1,)), ((), ())), preferred_element_type=jnp.float32)

def composite_grads(sigma, colors, spacing, ray_index, cotangent):
    ray_count = cotangent.shape[1]
    count = ray_index.shape[0]
    ray_numbers = jnp.arange(ray_count, dtype=jnp.int32)
    onehot = (ray_index[:, None] == ray_numbers[None, :]).astype(jnp.float32)
    positions = jnp.arange(count, dtype=jnp.int32)
    earlier = ((positions[:, None] < positions[None, :]) & (ray_index[:, None] == ray_index[None, :])).astype(jnp.float32)

    def render(density, shades):
        depth = density * spacing
        inside = jnp.dot(depth, earlier, precision=lax.Precision.HIGHEST)
        weight = jnp.exp(-inside) * -jnp.expm1(-depth)
        return jnp.dot(shades * weight[None, :], onehot, precision=lax.Precision.HIGHEST)
    _, pullback = jax.vjp(render, sigma, colors)
    return pullback(cotangent)

def head_backward(unscaled, gates, head_bias, spacing, ray_index, cotangent):
    logits = gates[:, None] * unscaled + head_bias[None, :]
    sigma = jax.nn.softplus(logits[:, 0])
    colors = jax.nn.sigmoid(logits[:, 1:])
    grad_sigma, grad_colors = composite_grads(sigma, colors.T, spacing, ray_index, cotangent)
    first = grad_sigma * jax.nn.sigmoid(logits[:, 0])
    others = grad_colors.T * colors * (1.0 - colors)
    return jnp.concatenate([first[:, None], others], axis=1)

def reference(inputs, layer_weights, layer_biases, head_weight, head_bias, gate_values, spacing, ray_index, expert_index, slot_index, color_cotangent):
    groups = REPLICAS * EXPERTS
    samples = SAMPLES_DEV
    flat_inputs = inputs.reshape(groups, samples, D)
    padded_inputs = jnp.concatenate([flat_inputs, jnp.zeros((groups, 1, D), flat_inputs.dtype)], axis=1)
    flat_experts = expert_index.reshape(groups, samples).astype(jnp.int32)
    flat_slots = slot_index.reshape(groups, samples).astype(jnp.int32)
    cell_index = flat_experts * CAP + flat_slots

    def invert(cells):
        return jnp.full((EXPERTS * CAP,), samples, jnp.int32).at[cells].set(jnp.arange(samples, dtype=jnp.int32))
    table = jax.vmap(invert)(cell_index).reshape(groups, EXPERTS, CAP)
    group_ids = jnp.arange(groups, dtype=jnp.int32)[:, None]

    def expert_rows(expert):
        picks = table[:, expert, :]
        rows = jnp.take_along_axis(padded_inputs, picks[:, :, None], axis=1)
        return (rows.reshape(groups * CAP, D), picks)

    def first_pass(expert):
        rows, _ = expert_rows(expert)
        _, features = forward(rows, layer_weights[expert], layer_biases[expert])
        return head_product(features, head_weight).reshape(groups, CAP, HEAD)
    unscaled_slots = lax.map(first_pass, jnp.arange(EXPERTS, dtype=jnp.int32))
    unscaled = unscaled_slots[flat_experts, group_ids, flat_slots]
    gates = gate_values.reshape(groups, samples)
    grad_logits = jax.vmap(head_backward, in_axes=(0, 0, None, 0, 0, 0))(unscaled, gates, head_bias, spacing.reshape(groups, samples), ray_index.reshape(groups, samples).astype(jnp.int32), color_cotangent.reshape(groups, 3, RAYS_DEV))
    scaled = gates[:, :, None] * grad_logits
    grad_head_bias = lax.optimization_barrier(jnp.sum(grad_logits, axis=(0, 1)))
    slot_grads = jnp.zeros((EXPERTS, groups, CAP, HEAD), jnp.float32).at[flat_experts, group_ids, flat_slots].set(scaled)
    head_float = head_weight.astype(jnp.float32)

    def second_pass(carry, expert):
        input_acc, head_acc = carry
        rows, picks = expert_rows(expert)
        activations, features = forward(rows, layer_weights[expert], layer_biases[expert])
        coming = slot_grads[expert].reshape(groups * CAP, HEAD)
        feature_grads = jnp.dot(coming, head_float, precision=lax.Precision.HIGHEST).astype(jnp.bfloat16)
        head_acc = head_acc + lax.dot_general(coming, features.astype(jnp.float32), (((0,), (0,)), ((), ())), precision=lax.Precision.HIGHEST)
        weight_grads, bias_grads, input_rows = backward(activations, layer_weights[expert], feature_grads)
        spread_ids = jnp.broadcast_to(group_ids, (groups, CAP))
        input_acc = input_acc.at[spread_ids, picks].set(input_rows.reshape(groups, CAP, D), mode='drop')
        return ((input_acc, head_acc), (weight_grads, bias_grads))
    start = (jnp.zeros((groups, samples, D), jnp.bfloat16), jnp.zeros((HEAD, D), jnp.float32))
    (input_acc, head_acc), (grad_weights, grad_biases) = lax.scan(second_pass, start, jnp.arange(EXPERTS, dtype=jnp.int32))
    grad_inputs = input_acc.reshape(REPLICAS, EXPERTS, samples, D)
    return (grad_inputs, grad_weights, grad_biases, head_acc, grad_head_bias)
```

```python
import functools

import jax
import jax.numpy as jnp
from jax import lax
from jax.experimental import pallas as pl
from jax.experimental.pallas import tpu as pltpu
from jax.sharding import PartitionSpec as P

MESH = pl.DeviceIdType.MESH
HIGHEST = lax.Precision.HIGHEST
F32 = jnp.float32
BF16 = jnp.bfloat16


def matmul(a, b, dims, precision=None):
    return lax.dot_general(
        a, b, (dims, ((), ())), precision=precision, preferred_element_type=F32
    )


def softplus(v):
    return jnp.maximum(v, 0.0) + jnp.log1p(jnp.exp(-jnp.abs(v)))


def sigmoid(v):
    small = jnp.exp(-jnp.abs(v))
    return jnp.where(v >= 0.0, 1.0, small) / (1.0 + small)


def one_minus_exp(t):
    series = t * (1.0 - t * (0.5 - t * (1.0 / 6.0 - t * (1.0 / 24.0 - t * (1.0 / 120.0)))))
    return jnp.where(t < 0.06, series, 1.0 - jnp.exp(-t))


def factors(experts):
    stages = []
    stride = 1
    for extent in (2, 4, 8):
        extent = min(extent, experts // stride)
        if extent > 1:
            stages.append((extent, stride))
            stride *= extent
    return stages


def composite(unscaled, gate, hb_ref, spacing, ray, ct_ref):
    rays = ct_ref.shape[1]
    samples = ray.shape[1]
    logits = [gate * unscaled[h : h + 1, :] + hb_ref[0:1, h : h + 1] for h in range(4)]
    sigma = softplus(logits[0])
    colors = [sigmoid(logits[h]) for h in range(1, 4)]
    tau = sigma * spacing
    hot = (lax.broadcasted_iota(jnp.int32, (8, samples), 0) == ray).astype(F32)
    same = matmul(hot.astype(BF16), hot.astype(BF16), ((0,), (0,)))
    before = lax.broadcasted_iota(jnp.int32, (samples, samples), 0)
    after = lax.broadcasted_iota(jnp.int32, (samples, samples), 1)
    earlier = jnp.where(before < after, same, 0.0)
    inside = matmul(jnp.broadcast_to(tau, (8, samples)), earlier, ((1,), (0,)), HIGHEST)[0:1, :]
    clear = jnp.exp(-inside)
    opacity = one_minus_exp(tau)
    weight = clear * opacity
    grads = []
    weight_grad = jnp.zeros_like(weight)
    for k in range(3):
        cotangent = jnp.zeros_like(weight)
        for r in range(rays):
            cotangent += ct_ref[k : k + 1, r : r + 1] * hot[r : r + 1, :]
        weight_grad += cotangent * colors[k]
        grads.append(cotangent * weight * colors[k] * (1.0 - colors[k]))
    inside_grad = -weight_grad * weight
    spread = matmul(
        jnp.broadcast_to(inside_grad, (8, samples)), earlier, ((1,), (1,)), HIGHEST
    )[0:1, :]
    tau_grad = weight_grad * clear * jnp.exp(-tau) + spread
    first = tau_grad * spacing * sigmoid(logits[0])
    return [first] + grads


def body(
    replicas,
    experts,
    in_ref,
    w_ref,
    b_ref,
    hw_ref,
    hb_ref,
    gate_ref,
    spacing_ref,
    ray_ref,
    expert_ref,
    slot_ref,
    ct_ref,
    out_in,
    out_w,
    out_small,
    acts,
    head_rows,
    row_send,
    row_recv,
    up_send,
    up_recv,
    down_send,
    down_recv,
    back_send,
    back_recv,
    part,
    chain_send,
    chain_recv,
    head_part,
    head_recv,
    small,
    small_recv,
    a2a_send_sem,
    a2a_recv_sem,
    chain_send_sem,
    chain_recv_sem,
    ring_send_sem,
    ring_recv_sem,
    head_send_sem,
    head_recv_sem,
    small_send_sem,
    small_recv_sem,
):
    samples, width = in_ref.shape
    layers = w_ref.shape[0]
    cap = 2 * samples // experts
    cells = experts * cap
    lanes = head_rows.shape[0]
    piece = width // replicas
    me_d = lax.axis_index("dp")
    me_e = lax.axis_index("expert")
    above = lax.rem(me_d + 1, replicas)
    below = lax.rem(me_d + replicas - 1, replicas)
    reach = (replicas // 2, replicas - 1 - replicas // 2)
    stages = factors(experts)

    barrier = pltpu.get_barrier_semaphore()

    def greet_e(k, c):
        pl.semaphore_signal(
            barrier, inc=1, device_id={"expert": lax.rem(me_e + k, experts)}, device_id_type=MESH
        )
        return c

    def greet_d(k, c):
        pl.semaphore_signal(
            barrier, inc=1, device_id={"dp": lax.rem(me_d + k, replicas)}, device_id_type=MESH
        )
        return c

    lax.fori_loop(1, experts, greet_e, 0)
    lax.fori_loop(1, replicas, greet_d, 0)

    def exchange(phase, source, target):
        def send(k, c):
            peer = lax.rem(me_e + k, experts)
            pltpu.make_async_remote_copy(
                src_ref=source.at[peer],
                dst_ref=target.at[me_e],
                send_sem=a2a_send_sem.at[phase],
                recv_sem=a2a_recv_sem.at[phase],
                device_id={"expert": peer},
                device_id_type=MESH,
            ).start()
            return c

        lax.fori_loop(1, experts, send, 0)
        target[me_e] = source[me_e]

    def arrive(phase, source, target):
        most = pl.ds(0, experts - 1)
        pltpu.make_async_copy(source.at[most], target.at[most], a2a_recv_sem.at[phase]).wait()

    def sent(phase, source, target):
        most = pl.ds(0, experts - 1)
        pltpu.make_async_copy(source.at[most], target.at[most], a2a_send_sem.at[phase]).wait()

    cell = expert_ref[...] * cap + slot_ref[...]
    pick = (lax.broadcasted_iota(jnp.int32, (cells, samples), 0) == cell).astype(BF16)
    rows = matmul(pick, in_ref[...], ((1,), (0,)))
    row_send[...] = rows.reshape(experts, cap, width).astype(BF16)
    head_rows[...] = jnp.zeros_like(head_rows)
    for h in range(4):
        head_rows[h * cap : (h + 1) * cap, :] = jnp.broadcast_to(
            hw_ref[h : h + 1, :].astype(F32), (cap, width)
        )
    pl.semaphore_wait(barrier, experts + replicas - 2)
    exchange(0, row_send, row_recv)
    arrive(0, row_send, row_recv)
    acts[0] = row_recv[...].astype(F32).reshape(cells, width).astype(BF16)

    def forward(layer, c):
        v = matmul(acts[layer], w_ref[layer], ((1,), (0,))) + b_ref[pl.ds(layer, 1), :]
        acts[layer + 1] = softplus(v).astype(BF16)
        return c

    lax.fori_loop(0, layers - 1, forward, 0)
    features = (
        matmul(acts[layers - 1], w_ref[layers - 1], ((1,), (0,))) + b_ref[layers - 1 : layers, :]
    ).astype(BF16)
    acts[layers] = features

    own_slot = lax.broadcasted_iota(jnp.int32, (cells, lanes), 0) % cap == (
        lax.broadcasted_iota(jnp.int32, (cells, lanes), 1) % cap
    )
    product = matmul(features, head_rows[...].astype(BF16), ((1,), (1,)))
    up_send[...] = (
        jnp.where(own_slot, product, 0.0).reshape(experts, cap, lanes).sum(axis=1, keepdims=True)
    )
    exchange(1, up_send, up_recv)
    arrive(1, up_send, up_recv)

    named = (lax.broadcasted_iota(jnp.int32, (experts, samples), 0) == expert_ref[...]).astype(F32)
    table = up_recv[...].reshape(experts, lanes)
    picked = matmul(table, named, ((0,), (0,)), HIGHEST)
    slot_hot = lax.broadcasted_iota(jnp.int32, (cap, samples), 0) == slot_ref[...]
    unscaled = jnp.concatenate(
        [
            jnp.where(slot_hot, picked[h * cap : (h + 1) * cap, :], 0.0).sum(axis=0, keepdims=True)
            for h in range(4)
        ],
        axis=0,
    )
    gate = gate_ref[...]
    grad_logits = composite(unscaled, gate, hb_ref, spacing_ref[...], ray_ref[...], ct_ref)
    placed = jnp.concatenate(
        [
            jnp.where(slot_hot, jnp.broadcast_to(gate * grad_logits[h], (cap, samples)), 0.0)
            for h in range(4)
        ]
        + [jnp.zeros((lanes - 4 * cap, samples), F32)],
        axis=0,
    )
    down_send[...] = matmul(named, placed, ((1,), (1,)), HIGHEST).reshape(experts, 1, lanes)
    exchange(2, down_send, down_recv)
    for h in range(4):
        head_part[4 + h : 5 + h, :] = jnp.broadcast_to(
            grad_logits[h].sum(axis=1, keepdims=True), (1, width)
        )
    arrive(2, down_send, down_recv)

    coming = jnp.where(
        own_slot,
        jnp.broadcast_to(down_recv[...], (experts, cap, lanes)).reshape(cells, lanes),
        0.0,
    )
    first_upstream = matmul(coming, head_rows[...], ((1,), (0,)), HIGHEST).astype(BF16)
    head_all = matmul(coming, acts[layers].astype(F32), ((0,), (0,)), HIGHEST)
    for h in range(4):
        head_part[h : h + 1, :] = head_all[h * cap : (h + 1) * cap, :].sum(axis=0, keepdims=True)
    acts[layers] = first_upstream

    def head_peer(stage, k):
        extent, stride = stages[stage]
        mine = lax.rem(me_e // stride, extent)
        return mine, me_e + (lax.rem(mine + k, extent) - mine) * stride

    def head_start(stage):
        extent, stride = stages[stage]
        mine, _ = head_peer(stage, 0)
        head_recv[stage, mine] = head_part[...]
        for k in range(1, extent):
            pltpu.make_async_remote_copy(
                src_ref=head_part,
                dst_ref=head_recv.at[stage, mine],
                send_sem=head_send_sem.at[stage],
                recv_sem=head_recv_sem.at[stage],
                device_id={"expert": head_peer(stage, k)[1]},
                device_id_type=MESH,
            ).start()

    def head_finish(stage):
        extent, stride = stages[stage]
        block = head_recv.at[stage, pl.ds(0, extent - 1)]
        pltpu.make_async_copy(block, block, head_recv_sem.at[stage]).wait()
        pltpu.make_async_copy(block, block, head_send_sem.at[stage]).wait()
        total = head_recv[stage, 0]
        for k in range(1, extent):
            total = total + head_recv[stage, k]
        head_part[...] = total

    def chain_copy(way, layer, step):
        return pltpu.make_async_remote_copy(
            src_ref=chain_send.at[way, step, layer],
            dst_ref=chain_recv.at[way, step, layer],
            send_sem=chain_send_sem.at[way],
            recv_sem=chain_recv_sem.at[way, step, layer],
            device_id={"dp": below if way == 0 else above},
            device_id_type=MESH,
        )

    def shard_of(way, distance):
        if way == 0:
            return lax.rem(me_d + replicas - distance, replicas)
        return lax.rem(me_d + distance, replicas)

    def weight_grad(layer):
        upstream = acts[layers]
        part[layer] = matmul(acts[layer], upstream, ((0,), (0,))).reshape(replicas, piece, width)
        small[pl.ds(layer, 1), :] = upstream.astype(F32).sum(axis=0, keepdims=True)
        for way in range(2):
            if reach[way] > 0:
                chain_send[way, 0, layer] = part[layer, shard_of(way, reach[way])].astype(BF16)
                chain_copy(way, layer, 0).start()

    def backward(i, c):
        layer = layers - 1 - i
        weight_grad(layer)
        spread = matmul(acts[layers], w_ref[layer], ((1,), (1,)))
        acts[layers] = (spread * one_minus_exp(acts[layer].astype(F32))).astype(BF16)
        return c

    marks = [2, 4, layers - 1]
    head_start(0)
    done = 0
    for stage in range(3):
        lax.fori_loop(done, marks[stage], backward, 0)
        done = marks[stage]
        if stage < len(stages):
            head_finish(stage)
            if stage + 1 < len(stages):
                head_start(stage + 1)
    spread = matmul(acts[layers], w_ref[0], ((1,), (1,)))
    back_send[...] = spread.reshape(experts, cap, width).astype(BF16)
    exchange(3, back_send, back_recv)
    weight_grad(0)

    small[layers : layers + 8, :] = head_part[...]
    small_recv[me_d] = small[...]

    def small_start(k, c):
        peer = lax.rem(me_d + k, replicas)
        pltpu.make_async_remote_copy(
            src_ref=small,
            dst_ref=small_recv.at[me_d],
            send_sem=small_send_sem.at[0],
            recv_sem=small_recv_sem.at[0],
            device_id={"dp": peer},
            device_id_type=MESH,
        ).start()
        return c

    lax.fori_loop(1, replicas, small_start, 0)

    for step in range(1, max(reach)):

        def hop(i, c):
            layer = layers - 1 - i
            for way in range(2):
                if step < reach[way]:
                    chain_copy(way, layer, step - 1).wait_recv()
                    chain_send[way, step, layer] = (
                        chain_recv[way, step - 1, layer].astype(F32)
                        + part[layer, shard_of(way, reach[way] - step)]
                    ).astype(BF16)
                    chain_copy(way, layer, step).start()
            return c

        lax.fori_loop(0, layers, hop, 0)

    far = (reach[1], reach[0])

    def ring_copy(way, layer, step):
        owner = shard_of(1 - way, step)
        return pltpu.make_async_remote_copy(
            src_ref=out_w.at[owner, layer],
            dst_ref=out_w.at[owner, layer],
            send_sem=ring_send_sem.at[way],
            recv_sem=ring_recv_sem.at[way, step, layer],
            device_id={"dp": below if way == 0 else above},
            device_id_type=MESH,
        )

    def finish(i, c):
        layer = layers - 1 - i
        total = part[layer, me_d]
        for way in range(2):
            if reach[way] > 0:
                chain_copy(way, layer, reach[way] - 1).wait_recv()
                total = total + chain_recv[way, reach[way] - 1, layer].astype(F32)
        out_w[me_d, layer] = total.astype(BF16)
        for way in range(2):
            if far[way] > 0:
                ring_copy(way, layer, 0).start()
        return c

    lax.fori_loop(0, layers, finish, 0)
    for step in range(1, max(far)):

        def forward_on(i, c):
            layer = layers - 1 - i
            for way in range(2):
                if step < far[way]:
                    ring_arrive(way, layer, step - 1)
                    ring_copy(way, layer, step).start()
            return c

        def ring_arrive(way, layer, step):
            owner = shard_of(1 - way, step + 1)
            pltpu.make_async_copy(
                out_w.at[owner, layer], out_w.at[owner, layer], ring_recv_sem.at[way, step, layer]
            ).wait()

        lax.fori_loop(0, layers, forward_on, 0)

    arrive(3, back_send, back_recv)
    slots = back_recv[...].astype(F32).reshape(cells, width).astype(BF16)
    again = (lax.broadcasted_iota(jnp.int32, (cells, samples), 0) == cell).astype(BF16)
    out_in[...] = matmul(again, slots, ((0,), (0,))).astype(BF16)

    block = small_recv.at[pl.ds(0, replicas - 1)]
    pltpu.make_async_copy(block, block, small_recv_sem.at[0]).wait()
    total = small_recv[0]
    for k in range(1, replicas):
        total = total + small_recv[k]
    out_small[...] = total

    def last(i, c):
        layer = layers - 1 - i
        for way in range(2):
            if far[way] > 0:
                owner = shard_of(1 - way, far[way])
                pltpu.make_async_copy(
                    out_w.at[owner, layer],
                    out_w.at[owner, layer],
                    ring_recv_sem.at[way, far[way] - 1, layer],
                ).wait()
        return c

    lax.fori_loop(0, layers, last, 0)

    sent(0, row_send, row_recv)
    sent(1, up_send, up_recv)
    sent(2, down_send, down_recv)
    sent(3, back_send, back_recv)
    pltpu.make_async_copy(block, block, small_send_sem.at[0]).wait()
    for way in range(2):
        if reach[way] > 0:
            gone = chain_send.at[way, pl.ds(0, reach[way])]
            pltpu.make_async_copy(gone, gone, chain_send_sem.at[way]).wait()
        if far[way] > 0:
            gone = out_w.at[pl.ds(0, far[way])]
            pltpu.make_async_copy(gone, gone, ring_send_sem.at[way]).wait()


def per_device(
    replicas,
    experts,
    inputs,
    layer_weights,
    layer_biases,
    head_weight,
    head_bias,
    gate_values,
    spacing,
    ray_index,
    expert_index,
    slot_index,
    color_cotangent,
):
    samples, width = inputs.shape[2:]
    layers = layer_weights.shape[1]
    cap = 2 * samples // experts
    cells = experts * cap
    piece = width // replicas
    steps = replicas // 2
    lanes = 128
    dma = pltpu.SemaphoreType.DMA
    whole = pl.BlockSpec(memory_space=pltpu.VMEM)
    out_in, out_w, out_small = pl.pallas_call(
        functools.partial(body, replicas, experts),
        out_shape=(
            jax.ShapeDtypeStruct((samples, width), BF16),
            jax.ShapeDtypeStruct((replicas, layers, piece, width), BF16),
            jax.ShapeDtypeStruct((layers + 8, width), F32),
        ),
        in_specs=[whole] * 11,
        out_specs=(whole,) * 3,
        scratch_shapes=[
            pltpu.VMEM((layers + 1, cells, width), BF16),
            pltpu.VMEM((lanes, width), F32),
            pltpu.VMEM((experts, cap, width), BF16),
            pltpu.VMEM((experts, cap, width), BF16),
            pltpu.VMEM((experts, 1, lanes), F32),
            pltpu.VMEM((experts, 1, lanes), F32),
            pltpu.VMEM((experts, 1, lanes), F32),
            pltpu.VMEM((experts, 1, lanes), F32),
            pltpu.VMEM((experts, cap, width), BF16),
            pltpu.VMEM((experts, cap, width), BF16),
            pltpu.VMEM((layers, replicas, piece, width), F32),
            pltpu.VMEM((2, steps, layers, piece, width), BF16),
            pltpu.VMEM((2, steps, layers, piece, width), BF16),
            pltpu.VMEM((8, width), F32),
            pltpu.VMEM((3, 8, 8, width), F32),
            pltpu.VMEM((layers + 8, width), F32),
            pltpu.VMEM((replicas, layers + 8, width), F32),
            dma((4,)),
            dma((4,)),
            dma((2,)),
            dma((2, steps, layers)),
            dma((2,)),
            dma((2, steps, layers)),
            dma((3,)),
            dma((3,)),
            dma((1,)),
            dma((1,)),
        ],
        compiler_params=pltpu.CompilerParams(
            collective_id=0, has_side_effects=True, vmem_limit_bytes=56 * 1024 * 1024
        ),
    )(
        inputs.reshape(samples, width),
        layer_weights[0],
        layer_biases[0],
        head_weight,
        head_bias.reshape(1, 4),
        gate_values.reshape(1, samples),
        spacing.reshape(1, samples),
        ray_index.reshape(1, samples),
        expert_index.reshape(1, samples),
        slot_index.reshape(1, samples),
        color_cotangent.reshape(color_cotangent.shape[2:]),
    )
    grad_weights = out_w.transpose(1, 0, 2, 3).reshape(1, layers, width, width).astype(F32)
    return (
        out_in.reshape(1, 1, samples, width),
        grad_weights,
        out_small[None, :layers],
        out_small[layers : layers + 4],
        out_small[layers + 4 :, 0],
    )


def solution(mesh):
    in_specs = (
        P("dp", "expert", None, None),
        P("expert", None, None, None),
        P("expert", None, None),
        P(),
        P(),
        P("dp", "expert", None),
        P("dp", "expert", None),
        P("dp", "expert", None),
        P("dp", "expert", None),
        P("dp", "expert", None),
        P("dp", "expert", None, None),
    )
    out_specs = (
        P("dp", "expert", None, None),
        P("expert", None, None, None),
        P("expert", None, None),
        P(),
        P(),
    )
    return jax.shard_map(
        functools.partial(per_device, mesh.shape["dp"], mesh.shape["expert"]),
        mesh=mesh,
        in_specs=in_specs,
        out_specs=out_specs,
        check_vma=False,
    )
```

```python
import functools

import jax
import jax.numpy as jnp
from jax import lax
from jax.experimental import pallas as pl
from jax.experimental.pallas import tpu as pltpu
from jax.sharding import PartitionSpec as P

MESH = pl.DeviceIdType.MESH
HIGHEST = lax.Precision.HIGHEST
F32 = jnp.float32
BF16 = jnp.bfloat16


def matmul(a, b, dims, precision=None):
    return lax.dot_general(
        a, b, (dims, ((), ())), precision=precision, preferred_element_type=F32
    )


def softplus(v):
    return jnp.maximum(v, 0.0) + jnp.log1p(jnp.exp(-jnp.abs(v)))


def sigmoid(v):
    small = jnp.exp(-jnp.abs(v))
    return jnp.where(v >= 0.0, 1.0, small) / (1.0 + small)


def one_minus_exp(t):
    series = t * (1.0 - t * (0.5 - t * (1.0 / 6.0 - t * (1.0 / 24.0 - t * (1.0 / 120.0)))))
    return jnp.where(t < 0.06, series, 1.0 - jnp.exp(-t))


def factors(experts):
    stages = []
    stride = 1
    for extent in (2, 4, 8):
        extent = min(extent, experts // stride)
        if extent > 1:
            stages.append((extent, stride))
            stride *= extent
    return stages


def composite(unscaled, gate, hb_ref, spacing, ray, ct_ref):
    rays = ct_ref.shape[2]
    samples = ray.shape[1]
    logits = [gate * unscaled[h : h + 1, :] + hb_ref[0:1, h : h + 1] for h in range(4)]
    sigma = softplus(logits[0])
    colors = [sigmoid(logits[h]) for h in range(1, 4)]
    tau = sigma * spacing
    hot = (lax.broadcasted_iota(jnp.int32, (8, samples), 0) == ray).astype(F32)
    same = matmul(hot.astype(BF16), hot.astype(BF16), ((0,), (0,)))
    before = lax.broadcasted_iota(jnp.int32, (samples, samples), 0)
    after = lax.broadcasted_iota(jnp.int32, (samples, samples), 1)
    earlier = jnp.where(before < after, same, 0.0)
    inside = matmul(jnp.broadcast_to(tau, (8, samples)), earlier, ((1,), (0,)), HIGHEST)[0:1, :]
    clear = jnp.exp(-inside)
    opacity = one_minus_exp(tau)
    weight = clear * opacity
    grads = []
    weight_grad = jnp.zeros_like(weight)
    for k in range(3):
        cotangent = jnp.zeros_like(weight)
        for r in range(rays):
            cotangent += ct_ref[k, 0:1, r : r + 1] * hot[r : r + 1, :]
        weight_grad += cotangent * colors[k]
        grads.append(cotangent * weight * colors[k] * (1.0 - colors[k]))
    inside_grad = -weight_grad * weight
    spread = matmul(
        jnp.broadcast_to(inside_grad, (8, samples)), earlier, ((1,), (1,)), HIGHEST
    )[0:1, :]
    tau_grad = weight_grad * clear * jnp.exp(-tau) + spread
    first = tau_grad * spacing * sigmoid(logits[0])
    return [first] + grads


def body(
    replicas,
    experts,
    *refs,
):
    sources, refs = refs[:11], refs[11:]
    (out_in, out_w, out_small), refs = refs[:3], refs[3:]
    loaded, (load_sem, *refs) = refs[:11], refs[11:]
    loads = [pltpu.make_async_copy(a, b, load_sem.at[n]) for n, (a, b) in enumerate(zip(sources, loaded))]
    for load in loads:
        load.start()
    compute(replicas, experts, loads, *loaded, out_in, out_w, out_small, *refs)


def compute(
    replicas,
    experts,
    loads,
    in_ref,
    w_ref,
    b_ref,
    hw_ref,
    hb_ref,
    gate_ref,
    spacing_ref,
    ray_ref,
    expert_ref,
    slot_ref,
    ct_ref,
    out_in,
    out_w,
    out_small,
    acts,
    head_rows,
    row_send,
    row_recv,
    up_send,
    up_recv,
    down_send,
    down_recv,
    back_send,
    back_recv,
    part,
    chain_send,
    chain_recv,
    head_part,
    head_recv,
    small,
    small_recv,
    a2a_send_sem,
    a2a_recv_sem,
    chain_send_sem,
    chain_recv_sem,
    ring_send_sem,
    ring_recv_sem,
    head_send_sem,
    head_recv_sem,
    small_send_sem,
    small_recv_sem,
):
    samples, width = in_ref.shape
    layers = w_ref.shape[0]
    cap = 2 * samples // experts
    cells = experts * cap
    lanes = head_rows.shape[0]
    piece = width // replicas
    me_d = lax.axis_index("dp")
    me_e = lax.axis_index("expert")
    above = lax.rem(me_d + 1, replicas)
    below = lax.rem(me_d + replicas - 1, replicas)
    most = replicas // 2

    def reach(way, layer):
        return most - (layer + way) % 2

    stages = factors(experts)

    barrier = pltpu.get_barrier_semaphore()

    def greet_e(k, c):
        pl.semaphore_signal(
            barrier, inc=1, device_id={"expert": lax.rem(me_e + k, experts)}, device_id_type=MESH
        )
        return c

    def greet_d(k, c):
        pl.semaphore_signal(
            barrier, inc=1, device_id={"dp": lax.rem(me_d + k, replicas)}, device_id_type=MESH
        )
        return c

    lax.fori_loop(1, experts, greet_e, 0)
    lax.fori_loop(1, replicas, greet_d, 0)

    def exchange(phase, source, target):
        def send(k, c):
            peer = lax.rem(me_e + k, experts)
            pltpu.make_async_remote_copy(
                src_ref=source.at[peer],
                dst_ref=target.at[me_e],
                send_sem=a2a_send_sem.at[phase],
                recv_sem=a2a_recv_sem.at[phase],
                device_id={"expert": peer},
                device_id_type=MESH,
            ).start()
            return c

        lax.fori_loop(1, experts, send, 0)
        target[me_e] = source[me_e]

    def arrive(phase, source, target):
        peers = pl.ds(0, experts - 1)
        pltpu.make_async_copy(source.at[peers], target.at[peers], a2a_recv_sem.at[phase]).wait()

    def sent(phase, source, target):
        peers = pl.ds(0, experts - 1)
        pltpu.make_async_copy(source.at[peers], target.at[peers], a2a_send_sem.at[phase]).wait()

    for n in (0, 3, 8, 9):
        loads[n].wait()
    cell = expert_ref[...] * cap + slot_ref[...]
    pick = (lax.broadcasted_iota(jnp.int32, (cells, samples), 0) == cell).astype(BF16)
    rows = matmul(pick, in_ref[...], ((1,), (0,)))
    row_send[...] = rows.reshape(experts, cap, width).astype(BF16)
    head_rows[...] = jnp.zeros_like(head_rows)
    for h in range(4):
        head_rows[h * cap : (h + 1) * cap, :] = jnp.broadcast_to(
            hw_ref[h : h + 1, :].astype(F32), (cap, width)
        )
    pl.semaphore_wait(barrier, experts + replicas - 2)
    exchange(0, row_send, row_recv)
    arrive(0, row_send, row_recv)
    acts[0] = row_recv[...].astype(F32).reshape(cells, width).astype(BF16)

    for n in (1, 2, 4, 5, 6, 7, 10):
        loads[n].wait()

    def forward(layer, c):
        v = matmul(acts[layer], w_ref[layer], ((1,), (0,))) + b_ref[pl.ds(layer, 1), :]
        acts[layer + 1] = softplus(v).astype(BF16)
        return c

    lax.fori_loop(0, layers - 1, forward, 0)
    features = (
        matmul(acts[layers - 1], w_ref[layers - 1], ((1,), (0,))) + b_ref[layers - 1 : layers, :]
    ).astype(BF16)
    acts[layers] = features

    own_slot = lax.broadcasted_iota(jnp.int32, (cells, lanes), 0) % cap == (
        lax.broadcasted_iota(jnp.int32, (cells, lanes), 1) % cap
    )
    product = matmul(features, head_rows[...].astype(BF16), ((1,), (1,)))
    up_send[...] = (
        jnp.where(own_slot, product, 0.0).reshape(experts, cap, lanes).sum(axis=1, keepdims=True)
    )
    exchange(1, up_send, up_recv)
    arrive(1, up_send, up_recv)

    named = (lax.broadcasted_iota(jnp.int32, (experts, samples), 0) == expert_ref[...]).astype(F32)
    table = up_recv[...].reshape(experts, lanes)
    picked = matmul(table, named, ((0,), (0,)), HIGHEST)
    slot_hot = lax.broadcasted_iota(jnp.int32, (cap, samples), 0) == slot_ref[...]
    unscaled = jnp.concatenate(
        [
            jnp.where(slot_hot, picked[h * cap : (h + 1) * cap, :], 0.0).sum(axis=0, keepdims=True)
            for h in range(4)
        ],
        axis=0,
    )
    gate = gate_ref[...]
    grad_logits = composite(unscaled, gate, hb_ref, spacing_ref[...], ray_ref[...], ct_ref)
    placed = jnp.concatenate(
        [
            jnp.where(slot_hot, jnp.broadcast_to(gate * grad_logits[h], (cap, samples)), 0.0)
            for h in range(4)
        ]
        + [jnp.zeros((lanes - 4 * cap, samples), F32)],
        axis=0,
    )
    down_send[...] = matmul(named, placed, ((1,), (1,)), HIGHEST).reshape(experts, 1, lanes)
    exchange(2, down_send, down_recv)
    for h in range(4):
        head_part[4 + h : 5 + h, :] = jnp.broadcast_to(
            grad_logits[h].sum(axis=1, keepdims=True), (1, width)
        )
    arrive(2, down_send, down_recv)

    coming = jnp.where(
        own_slot,
        jnp.broadcast_to(down_recv[...], (experts, cap, lanes)).reshape(cells, lanes),
        0.0,
    )
    first_upstream = matmul(coming, head_rows[...], ((1,), (0,)), HIGHEST).astype(BF16)
    head_all = matmul(coming, acts[layers].astype(F32), ((0,), (0,)), HIGHEST)
    for h in range(4):
        head_part[h : h + 1, :] = head_all[h * cap : (h + 1) * cap, :].sum(axis=0, keepdims=True)
    acts[layers] = first_upstream

    def head_peer(stage, k):
        extent, stride = stages[stage]
        mine = lax.rem(me_e // stride, extent)
        return mine, me_e + (lax.rem(mine + k, extent) - mine) * stride

    def head_start(stage):
        extent, stride = stages[stage]
        mine, _ = head_peer(stage, 0)
        head_recv[stage, mine] = head_part[...]
        for k in range(1, extent):
            pltpu.make_async_remote_copy(
                src_ref=head_part,
                dst_ref=head_recv.at[stage, mine],
                send_sem=head_send_sem.at[stage],
                recv_sem=head_recv_sem.at[stage],
                device_id={"expert": head_peer(stage, k)[1]},
                device_id_type=MESH,
            ).start()

    def head_finish(stage):
        extent, stride = stages[stage]
        block = head_recv.at[stage, pl.ds(0, extent - 1)]
        pltpu.make_async_copy(block, block, head_recv_sem.at[stage]).wait()
        pltpu.make_async_copy(block, block, head_send_sem.at[stage]).wait()
        total = head_recv[stage, 0]
        for k in range(1, extent):
            total = total + head_recv[stage, k]
        head_part[...] = total

    def chain_copy(way, layer, step):
        return pltpu.make_async_remote_copy(
            src_ref=chain_send.at[way, step * layers + layer],
            dst_ref=chain_recv.at[way, step, layer],
            send_sem=chain_send_sem.at[way],
            recv_sem=chain_recv_sem.at[way, step, layer],
            device_id={"dp": below if way == 0 else above},
            device_id_type=MESH,
        )

    def shard_of(way, distance):
        if way == 0:
            return lax.rem(me_d + replicas - distance, replicas)
        return lax.rem(me_d + distance, replicas)

    def weight_grad(layer):
        upstream = acts[layers]
        part[layer] = matmul(acts[layer], upstream, ((0,), (0,))).reshape(replicas, piece, width)
        small[pl.ds(layer, 1), :] = upstream.astype(F32).sum(axis=0, keepdims=True)
        for way in range(2):
            chain_send[way, layer] = part[layer, shard_of(way, reach(way, layer))].astype(BF16)
            chain_copy(way, layer, 0).start()

    def backward(i, c):
        layer = layers - 1 - i
        weight_grad(layer)
        spread = matmul(acts[layers], w_ref[layer], ((1,), (1,)))
        acts[layers] = (spread * one_minus_exp(acts[layer].astype(F32))).astype(BF16)
        return c

    marks = [2, 4, layers - 1]
    head_start(0)
    done = 0
    for stage in range(3):
        lax.fori_loop(done, marks[stage], backward, 0)
        done = marks[stage]
        if stage < len(stages):
            head_finish(stage)
            if stage + 1 < len(stages):
                head_start(stage + 1)
    spread = matmul(acts[layers], w_ref[0], ((1,), (1,)))
    back_send[...] = spread.reshape(experts, cap, width).astype(BF16)
    exchange(3, back_send, back_recv)
    weight_grad(0)

    small[layers : layers + 8, :] = head_part[...]
    small_recv[me_d] = small[...]

    def small_start(k, c):
        peer = lax.rem(me_d + k, replicas)
        pltpu.make_async_remote_copy(
            src_ref=small,
            dst_ref=small_recv.at[me_d],
            send_sem=small_send_sem.at[0],
            recv_sem=small_recv_sem.at[0],
            device_id={"dp": peer},
            device_id_type=MESH,
        ).start()
        return c

    lax.fori_loop(1, replicas, small_start, 0)

    def by_pairs(step_of):
        def pair(i, c):
            for odd in (1, 0):
                step_of(layers - 2 - 2 * i + odd, odd)
            return c

        lax.fori_loop(0, layers // 2, pair, 0)

    for step in range(1, most):

        def hop(layer, odd):
            for way in range(2):
                if step < reach(way, odd):
                    chain_copy(way, layer, step - 1).wait_recv()
                    chain_send[way, step * layers + layer] = (
                        chain_recv[way, step - 1, layer].astype(F32)
                        + part[layer, shard_of(way, reach(way, odd) - step)]
                    ).astype(BF16)
                    chain_copy(way, layer, step).start()

        by_pairs(hop)

    def ring_copy(way, layer, step):
        owner = shard_of(1 - way, step)
        return pltpu.make_async_remote_copy(
            src_ref=out_w.at[owner, layer],
            dst_ref=out_w.at[owner, layer],
            send_sem=ring_send_sem.at[way],
            recv_sem=ring_recv_sem.at[way, step, layer],
            device_id={"dp": below if way == 0 else above},
            device_id_type=MESH,
        )

    def ring_arrive(way, layer, step):
        owner = shard_of(1 - way, step + 1)
        pltpu.make_async_copy(
            out_w.at[owner, layer], out_w.at[owner, layer], ring_recv_sem.at[way, step, layer]
        ).wait()

    def finish(layer, odd):
        total = part[layer, me_d]
        for way in range(2):
            chain_copy(way, layer, reach(way, odd) - 1).wait_recv()
            total = total + chain_recv[way, reach(way, odd) - 1, layer].astype(F32)
        out_w[me_d, layer] = total.astype(BF16)
        for way in range(2):
            ring_copy(way, layer, 0).start()

    by_pairs(finish)
    for step in range(1, most):

        def forward_on(layer, odd):
            for way in range(2):
                if step < reach(way, odd):
                    ring_arrive(way, layer, step - 1)
                    ring_copy(way, layer, step).start()

        by_pairs(forward_on)

    arrive(3, back_send, back_recv)
    slots = back_recv[...].astype(F32).reshape(cells, width).astype(BF16)
    again = (lax.broadcasted_iota(jnp.int32, (cells, samples), 0) == cell).astype(BF16)
    out_in[...] = matmul(again, slots, ((0,), (0,))).astype(BF16)

    block = small_recv.at[pl.ds(0, replicas - 1)]
    pltpu.make_async_copy(block, block, small_recv_sem.at[0]).wait()
    total = small_recv[0]
    for k in range(1, replicas):
        total = total + small_recv[k]
    out_small[...] = total

    def last(layer, odd):
        for way in range(2):
            ring_arrive(way, layer, reach(way, odd) - 1)

    by_pairs(last)

    sent(0, row_send, row_recv)
    sent(1, up_send, up_recv)
    sent(2, down_send, down_recv)
    sent(3, back_send, back_recv)
    pltpu.make_async_copy(block, block, small_send_sem.at[0]).wait()
    for way in range(2):
        gone = chain_send.at[way, pl.ds(0, most * layers - layers // 2)]
        pltpu.make_async_copy(gone, gone, chain_send_sem.at[way]).wait()
        pltpu.make_async_copy(gone, gone, ring_send_sem.at[way]).wait()


def write_out(
    in_ref, w_ref, small_ref, out_in, out_w, out_b, out_hw, out_hb, wide, out_sem
):
    layers = wide.shape[0]
    stores = [
        pltpu.make_async_copy(wide.at[n], out_w.at[n], out_sem.at[n]) for n in range(layers)
    ]
    for n in range(layers):
        wide[n] = w_ref[:, n].astype(F32)
        stores[n].start()
    out_in[...] = in_ref[...]
    out_b[...] = small_ref[0:layers, :]
    out_hw[...] = small_ref[layers : layers + 4, :]
    for h in range(4):
        out_hb[0:1, h : h + 1] = small_ref[layers + 4 + h : layers + 5 + h, 0:1]
    for store in stores:
        store.wait()


def per_device(
    replicas,
    experts,
    inputs,
    layer_weights,
    layer_biases,
    head_weight,
    head_bias,
    gate_values,
    spacing,
    ray_index,
    expert_index,
    slot_index,
    color_cotangent,
):
    samples, width = inputs.shape[2:]
    layers = layer_weights.shape[1]
    cap = 2 * samples // experts
    cells = experts * cap
    piece = width // replicas
    steps = replicas // 2
    lanes = 128
    dma = pltpu.SemaphoreType.DMA
    operands = (
        inputs.reshape(samples, width),
        layer_weights[0],
        layer_biases[0],
        head_weight,
        head_bias.reshape(1, 4),
        gate_values.reshape(1, samples),
        spacing.reshape(1, samples),
        ray_index.reshape(1, samples),
        expert_index.reshape(1, samples),
        slot_index.reshape(1, samples),
        color_cotangent.reshape(3, 1, color_cotangent.shape[3]),
    )
    whole = pl.BlockSpec(memory_space=pltpu.VMEM)
    out_in, out_w, out_small = pl.pallas_call(
        functools.partial(body, replicas, experts),
        out_shape=(
            jax.ShapeDtypeStruct((samples, width), BF16),
            jax.ShapeDtypeStruct((replicas, layers, piece, width), BF16),
            jax.ShapeDtypeStruct((layers + 8, width), F32),
        ),
        in_specs=[pl.BlockSpec(memory_space=pltpu.HBM)] * 11,
        out_specs=(whole,) * 3,
        scratch_shapes=[
            *(pltpu.VMEM(a.shape, a.dtype) for a in operands),
            dma((11,)),
            pltpu.VMEM((layers + 1, cells, width), BF16),
            pltpu.VMEM((lanes, width), F32),
            pltpu.VMEM((experts, cap, width), BF16),
            pltpu.VMEM((experts, cap, width), BF16),
            pltpu.VMEM((experts, 1, lanes), F32),
            pltpu.VMEM((experts, 1, lanes), F32),
            pltpu.VMEM((experts, 1, lanes), F32),
            pltpu.VMEM((experts, 1, lanes), F32),
            pltpu.VMEM((experts, cap, width), BF16),
            pltpu.VMEM((experts, cap, width), BF16),
            pltpu.VMEM((layers, replicas, piece, width), F32),
            pltpu.VMEM((2, steps * layers, piece, width), BF16),
            pltpu.VMEM((2, steps, layers, piece, width), BF16),
            pltpu.VMEM((8, width), F32),
            pltpu.VMEM((3, 8, 8, width), F32),
            pltpu.VMEM((layers + 8, width), F32),
            pltpu.VMEM((replicas, layers + 8, width), F32),
            dma((4,)),
            dma((4,)),
            dma((2,)),
            dma((2, steps, layers)),
            dma((2,)),
            dma((2, steps, layers)),
            dma((3,)),
            dma((3,)),
            dma((1,)),
            dma((1,)),
        ],
        compiler_params=pltpu.CompilerParams(
            collective_id=0, has_side_effects=True, vmem_limit_bytes=32 * 1024 * 1024
        ),
    )(*(pltpu.with_memory_space_constraint(a, pltpu.HBM) for a in operands))
    grad_inputs, grad_weights, grad_biases, grad_head_weight, grad_head_bias = pl.pallas_call(
        write_out,
        out_shape=(
            jax.ShapeDtypeStruct((samples, width), BF16),
            jax.ShapeDtypeStruct((layers, replicas, piece, width), F32),
            jax.ShapeDtypeStruct((layers, width), F32),
            jax.ShapeDtypeStruct((4, width), F32),
            jax.ShapeDtypeStruct((1, 4), F32),
        ),
        in_specs=[whole] * 3,
        out_specs=(whole, pl.BlockSpec(memory_space=pl.ANY), whole, whole, whole),
        scratch_shapes=[
            pltpu.VMEM((layers, replicas, piece, width), F32),
            dma((layers,)),
        ],
        compiler_params=pltpu.CompilerParams(vmem_limit_bytes=16 * 1024 * 1024),
    )(out_in, out_w, out_small)
    return (
        grad_inputs.reshape(1, 1, samples, width),
        grad_weights.reshape(1, layers, width, width),
        grad_biases[None],
        grad_head_weight,
        grad_head_bias.reshape(4),
    )


def solution(mesh):
    in_specs = (
        P("dp", "expert", None, None),
        P("expert", None, None, None),
        P("expert", None, None),
        P(),
        P(),
        P("dp", "expert", None),
        P("dp", "expert", None),
        P("dp", "expert", None),
        P("dp", "expert", None),
        P("dp", "expert", None),
        P("dp", "expert", None, None),
    )
    out_specs = (
        P("dp", "expert", None, None),
        P("expert", None, None, None),
        P("expert", None, None),
        P(),
        P(),
    )
    return jax.shard_map(
        functools.partial(per_device, mesh.shape["dp"], mesh.shape["expert"]),
        mesh=mesh,
        in_specs=in_specs,
        out_specs=out_specs,
        check_vma=False,
    )
```

```python
import functools

import jax
import jax.numpy as jnp
from jax import lax
from jax.experimental import pallas as pl
from jax.experimental.pallas import tpu as pltpu
from jax.sharding import PartitionSpec as P

MESH = pl.DeviceIdType.MESH
HIGHEST = lax.Precision.HIGHEST
F32 = jnp.float32
BF16 = jnp.bfloat16


def matmul(a, b, dims, precision=None):
    return lax.dot_general(
        a, b, (dims, ((), ())), precision=precision, preferred_element_type=F32
    )


def softplus(v):
    return jnp.maximum(v, 0.0) + jnp.log1p(jnp.exp(-jnp.abs(v)))


def sigmoid(v):
    small = jnp.exp(-jnp.abs(v))
    return jnp.where(v >= 0.0, 1.0, small) / (1.0 + small)


def one_minus_exp(t):
    series = t * (1.0 - t * (0.5 - t * (1.0 / 6.0 - t * (1.0 / 24.0 - t * (1.0 / 120.0)))))
    return jnp.where(t < 0.06, series, 1.0 - jnp.exp(-t))


def factors(experts):
    stages = []
    stride = 1
    for extent in (2, 4, 8):
        extent = min(extent, experts // stride)
        if extent > 1:
            stages.append((extent, stride))
            stride *= extent
    return stages


def composite(unscaled, gate, hb_ref, spacing, ray, ct_ref):
    rays = ct_ref.shape[2]
    samples = ray.shape[1]
    logits = [gate * unscaled[h : h + 1, :] + hb_ref[0:1, h : h + 1] for h in range(4)]
    sigma = softplus(logits[0])
    colors = [sigmoid(logits[h]) for h in range(1, 4)]
    tau = sigma * spacing
    hot = (lax.broadcasted_iota(jnp.int32, (8, samples), 0) == ray).astype(F32)
    same = matmul(hot.astype(BF16), hot.astype(BF16), ((0,), (0,)))
    before = lax.broadcasted_iota(jnp.int32, (samples, samples), 0)
    after = lax.broadcasted_iota(jnp.int32, (samples, samples), 1)
    earlier = jnp.where(before < after, same, 0.0)
    inside = matmul(jnp.broadcast_to(tau, (8, samples)), earlier, ((1,), (0,)), HIGHEST)[0:1, :]
    clear = jnp.exp(-inside)
    opacity = one_minus_exp(tau)
    weight = clear * opacity
    grads = []
    weight_grad = jnp.zeros_like(weight)
    for k in range(3):
        cotangent = jnp.zeros_like(weight)
        for r in range(rays):
            cotangent += ct_ref[k, 0:1, r : r + 1] * hot[r : r + 1, :]
        weight_grad += cotangent * colors[k]
        grads.append(cotangent * weight * colors[k] * (1.0 - colors[k]))
    inside_grad = -weight_grad * weight
    spread = matmul(
        jnp.broadcast_to(inside_grad, (8, samples)), earlier, ((1,), (1,)), HIGHEST
    )[0:1, :]
    tau_grad = weight_grad * clear * jnp.exp(-tau) + spread
    first = tau_grad * spacing * sigmoid(logits[0])
    return [first] + grads


def body(
    replicas,
    experts,
    *refs,
):
    sources, refs = refs[:11], refs[11:]
    (out_in, out_w, out_small), refs = refs[:3], refs[3:]
    loaded, (load_sem, *refs) = refs[:11], refs[11:]
    loads = [pltpu.make_async_copy(a, b, load_sem.at[n]) for n, (a, b) in enumerate(zip(sources, loaded))]
    for load in loads:
        load.start()
    compute(replicas, experts, loads, *loaded, out_in, out_w, out_small, *refs)


def compute(
    replicas,
    experts,
    loads,
    in_ref,
    w_ref,
    b_ref,
    hw_ref,
    hb_ref,
    gate_ref,
    spacing_ref,
    ray_ref,
    expert_ref,
    slot_ref,
    ct_ref,
    out_in,
    out_w,
    out_small,
    acts,
    head_rows,
    row_send,
    row_recv,
    up_send,
    up_recv,
    down_send,
    down_recv,
    back_send,
    back_recv,
    part,
    chain_send,
    chain_recv,
    head_part,
    head_recv,
    small,
    small_recv,
    a2a_send_sem,
    a2a_recv_sem,
    chain_send_sem,
    chain_recv_sem,
    ring_send_sem,
    ring_recv_sem,
    head_send_sem,
    head_recv_sem,
    small_send_sem,
    small_recv_sem,
):
    samples, width = in_ref.shape
    layers = w_ref.shape[0]
    cap = 2 * samples // experts
    cells = experts * cap
    lanes = head_rows.shape[0]
    piece = width // replicas
    me_d = lax.axis_index("dp")
    me_e = lax.axis_index("expert")
    above = lax.rem(me_d + 1, replicas)
    below = lax.rem(me_d + replicas - 1, replicas)
    most = replicas // 2

    def reach(way, layer):
        return most - (layer + way) % 2

    stages = factors(experts)

    barrier = pltpu.get_barrier_semaphore()

    def greet_e(k, c):
        pl.semaphore_signal(
            barrier, inc=1, device_id={"expert": lax.rem(me_e + k, experts)}, device_id_type=MESH
        )
        return c

    def greet_d(k, c):
        pl.semaphore_signal(
            barrier, inc=1, device_id={"dp": lax.rem(me_d + k, replicas)}, device_id_type=MESH
        )
        return c

    lax.fori_loop(1, experts, greet_e, 0)
    lax.fori_loop(1, replicas, greet_d, 0)

    def exchange(phase, source, target):
        def send(k, c):
            exchange_one(phase, source, target, k)
            return c

        lax.fori_loop(1, experts, send, 0)
        target[me_e] = source[me_e]

    def exchange_one(phase, source, target, k):
        ahead = experts // 2 - k // 2
        peer = lax.rem(me_e + experts + ahead * (1 - 2 * (k % 2)), experts)
        pltpu.make_async_remote_copy(
            src_ref=source.at[peer],
            dst_ref=target.at[me_e],
            send_sem=a2a_send_sem.at[phase],
            recv_sem=a2a_recv_sem.at[phase],
            device_id={"expert": peer},
            device_id_type=MESH,
        ).start()

    def arrive(phase, source, target):
        peers = pl.ds(0, experts - 1)
        pltpu.make_async_copy(source.at[peers], target.at[peers], a2a_recv_sem.at[phase]).wait()

    def sent(phase, source, target):
        peers = pl.ds(0, experts - 1)
        pltpu.make_async_copy(source.at[peers], target.at[peers], a2a_send_sem.at[phase]).wait()

    for n in (0, 3, 8, 9):
        loads[n].wait()
    cell = expert_ref[...] * cap + slot_ref[...]
    pick = (lax.broadcasted_iota(jnp.int32, (cells, samples), 0) == cell).astype(BF16)
    rows = matmul(pick, in_ref[...], ((1,), (0,)))
    row_send[...] = rows.reshape(experts, cap, width).astype(BF16)
    head_rows[...] = jnp.zeros_like(head_rows)
    for h in range(4):
        head_rows[h * cap : (h + 1) * cap, :] = jnp.broadcast_to(
            hw_ref[h : h + 1, :].astype(F32), (cap, width)
        )
    pl.semaphore_wait(barrier, experts + replicas - 2)
    exchange(0, row_send, row_recv)
    arrive(0, row_send, row_recv)
    acts[0] = row_recv[...].astype(F32).reshape(cells, width).astype(BF16)

    for n in (1, 2, 4, 5, 6, 7, 10):
        loads[n].wait()

    def forward(layer, c):
        v = matmul(acts[layer], w_ref[layer], ((1,), (0,))) + b_ref[pl.ds(layer, 1), :]
        acts[layer + 1] = softplus(v).astype(BF16)
        return c

    lax.fori_loop(0, layers - 1, forward, 0)
    features = (
        matmul(acts[layers - 1], w_ref[layers - 1], ((1,), (0,))) + b_ref[layers - 1 : layers, :]
    ).astype(BF16)
    acts[layers] = features

    own_slot = lax.broadcasted_iota(jnp.int32, (cells, lanes), 0) % cap == (
        lax.broadcasted_iota(jnp.int32, (cells, lanes), 1) % cap
    )
    product = matmul(features, head_rows[...].astype(BF16), ((1,), (1,)))
    up_send[...] = (
        jnp.where(own_slot, product, 0.0).reshape(experts, cap, lanes).sum(axis=1, keepdims=True)
    )
    exchange(1, up_send, up_recv)
    arrive(1, up_send, up_recv)

    named = (lax.broadcasted_iota(jnp.int32, (experts, samples), 0) == expert_ref[...]).astype(F32)
    table = up_recv[...].reshape(experts, lanes)
    picked = matmul(table, named, ((0,), (0,)), HIGHEST)
    slot_hot = lax.broadcasted_iota(jnp.int32, (cap, samples), 0) == slot_ref[...]
    unscaled = jnp.concatenate(
        [
            jnp.where(slot_hot, picked[h * cap : (h + 1) * cap, :], 0.0).sum(axis=0, keepdims=True)
            for h in range(4)
        ],
        axis=0,
    )
    gate = gate_ref[...]
    grad_logits = composite(unscaled, gate, hb_ref, spacing_ref[...], ray_ref[...], ct_ref)
    placed = jnp.concatenate(
        [
            jnp.where(slot_hot, jnp.broadcast_to(gate * grad_logits[h], (cap, samples)), 0.0)
            for h in range(4)
        ]
        + [jnp.zeros((lanes - 4 * cap, samples), F32)],
        axis=0,
    )
    down_send[...] = matmul(named, placed, ((1,), (1,)), HIGHEST).reshape(experts, 1, lanes)
    exchange(2, down_send, down_recv)
    for h in range(4):
        head_part[4 + h : 5 + h, :] = jnp.broadcast_to(
            grad_logits[h].sum(axis=1, keepdims=True), (1, width)
        )
    arrive(2, down_send, down_recv)

    coming = jnp.where(
        own_slot,
        jnp.broadcast_to(down_recv[...], (experts, cap, lanes)).reshape(cells, lanes),
        0.0,
    )
    first_upstream = matmul(coming, head_rows[...], ((1,), (0,)), HIGHEST).astype(BF16)
    head_all = matmul(coming, acts[layers].astype(F32), ((0,), (0,)), HIGHEST)
    for h in range(4):
        head_part[h : h + 1, :] = head_all[h * cap : (h + 1) * cap, :].sum(axis=0, keepdims=True)
    acts[layers] = first_upstream

    def head_peer(stage, k):
        extent, stride = stages[stage]
        mine = lax.rem(me_e // stride, extent)
        return mine, me_e + (lax.rem(mine + k, extent) - mine) * stride

    def head_start(stage):
        extent, stride = stages[stage]
        mine, _ = head_peer(stage, 0)
        head_recv[stage, mine] = head_part[...]
        for k in range(1, extent):
            pltpu.make_async_remote_copy(
                src_ref=head_part,
                dst_ref=head_recv.at[stage, mine],
                send_sem=head_send_sem.at[stage],
                recv_sem=head_recv_sem.at[stage],
                device_id={"expert": head_peer(stage, k)[1]},
                device_id_type=MESH,
            ).start()

    def head_finish(stage):
        extent, stride = stages[stage]
        block = head_recv.at[stage, pl.ds(0, extent - 1)]
        pltpu.make_async_copy(block, block, head_recv_sem.at[stage]).wait()
        pltpu.make_async_copy(block, block, head_send_sem.at[stage]).wait()
        total = head_recv[stage, 0]
        for k in range(1, extent):
            total = total + head_recv[stage, k]
        head_part[...] = total

    def chain_copy(way, layer, step):
        return pltpu.make_async_remote_copy(
            src_ref=chain_send.at[way, step * layers + layer],
            dst_ref=chain_recv.at[way, step, layer],
            send_sem=chain_send_sem.at[way],
            recv_sem=chain_recv_sem.at[way, step, layer],
            device_id={"dp": below if way == 0 else above},
            device_id_type=MESH,
        )

    def shard_of(way, distance):
        if way == 0:
            return lax.rem(me_d + replicas - distance, replicas)
        return lax.rem(me_d + distance, replicas)

    def weight_grad(layer):
        upstream = acts[layers]
        part[layer] = matmul(acts[layer], upstream, ((0,), (0,))).reshape(replicas, piece, width)
        small[lax.rem(layer, replicas), pl.ds(layer // replicas, 1), :] = upstream.astype(F32).sum(
            axis=0, keepdims=True
        )
        for way in range(2):
            chain_send[way, layer] = part[layer, shard_of(way, reach(way, layer))].astype(BF16)
            chain_copy(way, layer, 0).start()

    def hop(step, layer, way):
        chain_copy(way, layer, step - 1).wait_recv()
        chain_send[way, step * layers + layer] = (
            chain_recv[way, step - 1, layer].astype(F32)
            + part[layer, shard_of(way, reach(way, layer) - step)]
        ).astype(BF16)
        chain_copy(way, layer, step).start()

    lag = 3

    def hops(i, count):
        for step in range(1, most - 1):
            if step <= count:
                for way in range(2):
                    hop(step, layers - 1 - (i - lag * step), way)

    def backward_with(count):
        def backward(i, c):
            layer = layers - 1 - i
            weight_grad(layer)
            hops(i, count)
            spread = matmul(acts[layers], w_ref[layer], ((1,), (1,)))
            acts[layers] = (spread * one_minus_exp(acts[layer].astype(F32))).astype(BF16)
            return c

        return backward

    marks = [lag, 2 * lag, layers - 1]
    head_start(0)
    done = 0
    for stage in range(3):
        lax.fori_loop(done, marks[stage], backward_with(stage), 0)
        done = marks[stage]
        if stage < len(stages):
            head_finish(stage)
            if stage + 1 < len(stages):
                head_start(stage + 1)
    spread = matmul(acts[layers], w_ref[0], ((1,), (1,)))
    back_send[...] = spread.reshape(experts, cap, width).astype(BF16)
    back_recv[me_e] = back_send[me_e]
    weight_grad(0)
    hops(layers - 1, 2)

    for row in range(8):
        place = layers + row
        small[place % replicas, place // replicas : place // replicas + 1, :] = head_part[
            row : row + 1, :
        ]
    small_recv[me_d] = small[me_d]

    def small_start(k, c):
        peer = lax.rem(me_d + k, replicas)
        pltpu.make_async_remote_copy(
            src_ref=small.at[peer],
            dst_ref=small_recv.at[me_d],
            send_sem=small_send_sem.at[0],
            recv_sem=small_recv_sem.at[0],
            device_id={"dp": peer},
            device_id_type=MESH,
        ).start()
        return c

    lax.fori_loop(1, replicas, small_start, 0)

    work = sum(lag * step for step in range(1, most - 1)) + layers
    per_slot = pl.cdiv(experts - 1, work)

    def feed(slot):
        for n in range(per_slot):
            k = 1 + slot * per_slot + n

            @pl.when(k < experts)
            def _():
                exchange_one(3, back_send, back_recv, k)

    def by_pairs(step_of, first_slot=None):
        def pair(i, c):
            for odd in (1, 0):
                step_of(layers - 2 - 2 * i + odd, odd)
            if first_slot is not None:
                feed(first_slot + i)
            return c

        lax.fori_loop(0, layers // 2, pair, 0)

    slot = 0
    for step in range(1, most - 1):

        def remaining(i, c):
            for way in range(2):
                hop(step, layers - 1 - i, way)
            feed(slot + i - (layers - lag * step))
            return c

        begin = layers - lag * step
        lax.fori_loop(begin, layers, remaining, 0)
        slot += layers - begin

    def last_hop(layer, odd):
        for way in range(2):
            if most - 1 < reach(way, odd):
                hop(most - 1, layer, way)

    if most > 1:
        by_pairs(last_hop, slot)
        slot += layers // 2

    peers_d = small_recv.at[pl.ds(0, replicas - 1)]
    pltpu.make_async_copy(peers_d, peers_d, small_recv_sem.at[0]).wait()
    total = small_recv[0]
    for k in range(1, replicas):
        total = total + small_recv[k]
    out_small[me_d] = total

    def small_spread(k, c):
        pltpu.make_async_remote_copy(
            src_ref=out_small.at[me_d],
            dst_ref=out_small.at[me_d],
            send_sem=small_send_sem.at[1],
            recv_sem=small_recv_sem.at[1],
            device_id={"dp": lax.rem(me_d + k, replicas)},
            device_id_type=MESH,
        ).start()
        return c

    lax.fori_loop(1, replicas, small_spread, 0)

    def ring_copy(way, layer, step):
        owner = shard_of(1 - way, step)
        return pltpu.make_async_remote_copy(
            src_ref=out_w.at[owner, layer],
            dst_ref=out_w.at[owner, layer],
            send_sem=ring_send_sem.at[way],
            recv_sem=ring_recv_sem.at[way, step, layer],
            device_id={"dp": below if way == 0 else above},
            device_id_type=MESH,
        )

    def ring_arrive(way, layer, step):
        owner = shard_of(1 - way, step + 1)
        pltpu.make_async_copy(
            out_w.at[owner, layer], out_w.at[owner, layer], ring_recv_sem.at[way, step, layer]
        ).wait()

    def finish(layer, odd):
        total = part[layer, me_d]
        for way in range(2):
            chain_copy(way, layer, reach(way, odd) - 1).wait_recv()
            total = total + chain_recv[way, reach(way, odd) - 1, layer].astype(F32)
        out_w[me_d, layer] = total.astype(BF16)
        for way in range(2):
            ring_copy(way, layer, 0).start()

    by_pairs(finish, slot)
    for step in range(1, most):

        def forward_on(layer, odd):
            for way in range(2):
                if step < reach(way, odd):
                    ring_arrive(way, layer, step - 1)
                    ring_copy(way, layer, step).start()

        by_pairs(forward_on)

    arrive(3, back_send, back_recv)
    slots = back_recv[...].astype(F32).reshape(cells, width).astype(BF16)
    again = (lax.broadcasted_iota(jnp.int32, (cells, samples), 0) == cell).astype(BF16)
    out_in[...] = matmul(again, slots, ((0,), (0,))).astype(BF16)

    pltpu.make_async_copy(peers_d, peers_d, small_recv_sem.at[1]).wait()

    def last(layer, odd):
        for way in range(2):
            ring_arrive(way, layer, reach(way, odd) - 1)

    by_pairs(last)

    sent(0, row_send, row_recv)
    sent(1, up_send, up_recv)
    sent(2, down_send, down_recv)
    sent(3, back_send, back_recv)
    for n in range(2):
        pltpu.make_async_copy(peers_d, peers_d, small_send_sem.at[n]).wait()
    for way in range(2):
        gone = chain_send.at[way, pl.ds(0, most * layers - layers // 2)]
        pltpu.make_async_copy(gone, gone, chain_send_sem.at[way]).wait()
        pltpu.make_async_copy(gone, gone, ring_send_sem.at[way]).wait()


def write_out(
    in_ref, w_ref, small_ref, out_in, out_w, out_b, out_hw, out_hb, wide, out_sem
):
    layers = wide.shape[0]
    stores = [
        pltpu.make_async_copy(wide.at[n], out_w.at[n], out_sem.at[n]) for n in range(layers)
    ]
    for n in range(layers):
        wide[n] = w_ref[:, n].astype(F32)
        stores[n].start()
    out_in[...] = in_ref[...]
    replicas = small_ref.shape[0]

    def row(place):
        return small_ref[place % replicas, place // replicas : place // replicas + 1, :]

    for n in range(layers):
        out_b[n : n + 1, :] = row(n)
    for h in range(4):
        out_hw[h : h + 1, :] = row(layers + h)
        out_hb[0:1, h : h + 1] = row(layers + 4 + h)[:, 0:1]
    for store in stores:
        store.wait()


def per_device(
    replicas,
    experts,
    inputs,
    layer_weights,
    layer_biases,
    head_weight,
    head_bias,
    gate_values,
    spacing,
    ray_index,
    expert_index,
    slot_index,
    color_cotangent,
):
    samples, width = inputs.shape[2:]
    layers = layer_weights.shape[1]
    cap = 2 * samples // experts
    cells = experts * cap
    piece = width // replicas
    steps = replicas // 2
    lanes = 128
    dma = pltpu.SemaphoreType.DMA
    operands = (
        inputs.reshape(samples, width),
        layer_weights[0],
        layer_biases[0],
        head_weight,
        head_bias.reshape(1, 4),
        gate_values.reshape(1, samples),
        spacing.reshape(1, samples),
        ray_index.reshape(1, samples),
        expert_index.reshape(1, samples),
        slot_index.reshape(1, samples),
        color_cotangent.reshape(3, 1, color_cotangent.shape[3]),
    )
    whole = pl.BlockSpec(memory_space=pltpu.VMEM)
    out_in, out_w, out_small = pl.pallas_call(
        functools.partial(body, replicas, experts),
        out_shape=(
            jax.ShapeDtypeStruct((samples, width), BF16),
            jax.ShapeDtypeStruct((replicas, layers, piece, width), BF16),
            jax.ShapeDtypeStruct((replicas, (layers + 8) // replicas, width), F32),
        ),
        in_specs=[pl.BlockSpec(memory_space=pltpu.HBM)] * 11,
        out_specs=(whole,) * 3,
        scratch_shapes=[
            *(pltpu.VMEM(a.shape, a.dtype) for a in operands),
            dma((11,)),
            pltpu.VMEM((layers + 1, cells, width), BF16),
            pltpu.VMEM((lanes, width), F32),
            pltpu.VMEM((experts, cap, width), BF16),
            pltpu.VMEM((experts, cap, width), BF16),
            pltpu.VMEM((experts, 1, lanes), F32),
            pltpu.VMEM((experts, 1, lanes), F32),
            pltpu.VMEM((experts, 1, lanes), F32),
            pltpu.VMEM((experts, 1, lanes), F32),
            pltpu.VMEM((experts, cap, width), BF16),
            pltpu.VMEM((experts, cap, width), BF16),
            pltpu.VMEM((layers, replicas, piece, width), F32),
            pltpu.VMEM((2, steps * layers, piece, width), BF16),
            pltpu.VMEM((2, steps, layers, piece, width), BF16),
            pltpu.VMEM((8, width), F32),
            pltpu.VMEM((3, 8, 8, width), F32),
            pltpu.VMEM((replicas, (layers + 8) // replicas, width), F32),
            pltpu.VMEM((replicas, (layers + 8) // replicas, width), F32),
            dma((4,)),
            dma((4,)),
            dma((2,)),
            dma((2, steps, layers)),
            dma((2,)),
            dma((2, steps, layers)),
            dma((3,)),
            dma((3,)),
            dma((2,)),
            dma((2,)),
        ],
        compiler_params=pltpu.CompilerParams(
            collective_id=0, has_side_effects=True, vmem_limit_bytes=32 * 1024 * 1024
        ),
    )(*(pltpu.with_memory_space_constraint(a, pltpu.HBM) for a in operands))
    grad_inputs, grad_weights, grad_biases, grad_head_weight, grad_head_bias = pl.pallas_call(
        write_out,
        out_shape=(
            jax.ShapeDtypeStruct((samples, width), BF16),
            jax.ShapeDtypeStruct((layers, replicas, piece, width), F32),
            jax.ShapeDtypeStruct((layers, width), F32),
            jax.ShapeDtypeStruct((4, width), F32),
            jax.ShapeDtypeStruct((1, 4), F32),
        ),
        in_specs=[whole] * 3,
        out_specs=(whole, pl.BlockSpec(memory_space=pl.ANY), whole, whole, whole),
        scratch_shapes=[
            pltpu.VMEM((layers, replicas, piece, width), F32),
            dma((layers,)),
        ],
        compiler_params=pltpu.CompilerParams(vmem_limit_bytes=16 * 1024 * 1024),
    )(out_in, out_w, out_small)
    return (
        grad_inputs.reshape(1, 1, samples, width),
        grad_weights.reshape(1, layers, width, width),
        grad_biases[None],
        grad_head_weight,
        grad_head_bias.reshape(4),
    )


def solution(mesh):
    in_specs = (
        P("dp", "expert", None, None),
        P("expert", None, None, None),
        P("expert", None, None),
        P(),
        P(),
        P("dp", "expert", None),
        P("dp", "expert", None),
        P("dp", "expert", None),
        P("dp", "expert", None),
        P("dp", "expert", None),
        P("dp", "expert", None, None),
    )
    out_specs = (
        P("dp", "expert", None, None),
        P("expert", None, None, None),
        P("expert", None, None),
        P(),
        P(),
    )
    return jax.shard_map(
        functools.partial(per_device, mesh.shape["dp"], mesh.shape["expert"]),
        mesh=mesh,
        in_specs=in_specs,
        out_specs=out_specs,
        check_vma=False,
    )
```

```python
import functools

import jax
import jax.numpy as jnp
from jax import lax
from jax.experimental import pallas as pl
from jax.experimental.pallas import tpu as pltpu
from jax.sharding import PartitionSpec as P

MESH = pl.DeviceIdType.MESH
HIGHEST = lax.Precision.HIGHEST
F32 = jnp.float32
BF16 = jnp.bfloat16


def matmul(a, b, dims, precision=None):
    return lax.dot_general(
        a, b, (dims, ((), ())), precision=precision, preferred_element_type=F32
    )


def softplus(v):
    return jnp.maximum(v, 0.0) + jnp.log1p(jnp.exp(-jnp.abs(v)))


def sigmoid(v):
    small = jnp.exp(-jnp.abs(v))
    return jnp.where(v >= 0.0, 1.0, small) / (1.0 + small)


def one_minus_exp(t):
    series = t * (1.0 - t * (0.5 - t * (1.0 / 6.0 - t * (1.0 / 24.0 - t * (1.0 / 120.0)))))
    return jnp.where(t < 0.06, series, 1.0 - jnp.exp(-t))


def factors(experts):
    stages = []
    stride = 1
    for extent in (2, 4, 8):
        extent = min(extent, experts // stride)
        if extent > 1:
            stages.append((extent, stride))
            stride *= extent
    return stages


def composite(unscaled, gate, hb_ref, spacing, ray, ct_ref):
    rays = ct_ref.shape[2]
    samples = ray.shape[1]
    logits = [gate * unscaled[h : h + 1, :] + hb_ref[0:1, h : h + 1] for h in range(4)]
    sigma = softplus(logits[0])
    colors = [sigmoid(logits[h]) for h in range(1, 4)]
    tau = sigma * spacing
    hot = (lax.broadcasted_iota(jnp.int32, (8, samples), 0) == ray).astype(F32)
    same = matmul(hot.astype(BF16), hot.astype(BF16), ((0,), (0,)))
    before = lax.broadcasted_iota(jnp.int32, (samples, samples), 0)
    after = lax.broadcasted_iota(jnp.int32, (samples, samples), 1)
    earlier = jnp.where(before < after, same, 0.0)
    inside = matmul(jnp.broadcast_to(tau, (8, samples)), earlier, ((1,), (0,)), HIGHEST)[0:1, :]
    clear = jnp.exp(-inside)
    opacity = one_minus_exp(tau)
    weight = clear * opacity
    grads = []
    weight_grad = jnp.zeros_like(weight)
    for k in range(3):
        cotangent = jnp.zeros_like(weight)
        for r in range(rays):
            cotangent += ct_ref[k, 0:1, r : r + 1] * hot[r : r + 1, :]
        weight_grad += cotangent * colors[k]
        grads.append(cotangent * weight * colors[k] * (1.0 - colors[k]))
    inside_grad = -weight_grad * weight
    spread = matmul(
        jnp.broadcast_to(inside_grad, (8, samples)), earlier, ((1,), (1,)), HIGHEST
    )[0:1, :]
    tau_grad = weight_grad * clear * jnp.exp(-tau) + spread
    first = tau_grad * spacing * sigmoid(logits[0])
    return [first] + grads


def body(
    replicas,
    experts,
    *refs,
):
    sources, refs = refs[:11], refs[11:]
    (out_in, out_w, out_small), refs = refs[:3], refs[3:]
    loaded, (load_sem, *refs) = refs[:11], refs[11:]
    loads = [pltpu.make_async_copy(a, b, load_sem.at[n]) for n, (a, b) in enumerate(zip(sources, loaded))]
    for load in loads:
        load.start()
    compute(replicas, experts, loads, *loaded, out_in, out_w, out_small, *refs)


def compute(
    replicas,
    experts,
    loads,
    in_ref,
    w_ref,
    b_ref,
    hw_ref,
    hb_ref,
    gate_ref,
    spacing_ref,
    ray_ref,
    expert_ref,
    slot_ref,
    ct_ref,
    out_in,
    out_w,
    out_small,
    acts,
    head_rows,
    row_send,
    row_recv,
    up_send,
    up_recv,
    down_send,
    down_recv,
    back_send,
    back_recv,
    part,
    chain_send,
    chain_recv,
    head_part,
    head_recv,
    small,
    small_recv,
    a2a_send_sem,
    a2a_recv_sem,
    chain_send_sem,
    chain_recv_sem,
    ring_send_sem,
    ring_recv_sem,
    head_send_sem,
    head_recv_sem,
    small_send_sem,
    small_recv_sem,
):
    samples, width = in_ref.shape
    layers = w_ref.shape[0]
    cap = 2 * samples // experts
    cells = experts * cap
    lanes = head_rows.shape[0]
    piece = width // replicas
    me_d = lax.axis_index("dp")
    me_e = lax.axis_index("expert")
    above = lax.rem(me_d + 1, replicas)
    below = lax.rem(me_d + replicas - 1, replicas)
    most = replicas // 2

    def reach(way, layer):
        return most - (layer + way) % 2

    stages = factors(experts)

    barrier = pltpu.get_barrier_semaphore()

    def greet_e(k, c):
        pl.semaphore_signal(
            barrier, inc=1, device_id={"expert": lax.rem(me_e + k, experts)}, device_id_type=MESH
        )
        return c

    def greet_d(k, c):
        pl.semaphore_signal(
            barrier, inc=1, device_id={"dp": lax.rem(me_d + k, replicas)}, device_id_type=MESH
        )
        return c

    lax.fori_loop(1, experts, greet_e, 0)
    lax.fori_loop(1, replicas, greet_d, 0)

    def exchange(phase, source, target):
        def send(k, c):
            exchange_one(phase, source, target, k)
            return c

        lax.fori_loop(1, experts, send, 0)
        target[me_e] = source[me_e]

    def exchange_one(phase, source, target, k):
        ahead = experts // 2 - k // 2
        peer = lax.rem(me_e + experts + ahead * (1 - 2 * (k % 2)), experts)
        pltpu.make_async_remote_copy(
            src_ref=source.at[peer],
            dst_ref=target.at[me_e],
            send_sem=a2a_send_sem.at[phase],
            recv_sem=a2a_recv_sem.at[phase],
            device_id={"expert": peer},
            device_id_type=MESH,
        ).start()

    def arrive(phase, source, target):
        peers = pl.ds(0, experts - 1)
        pltpu.make_async_copy(source.at[peers], target.at[peers], a2a_recv_sem.at[phase]).wait()

    def sent(phase, source, target):
        peers = pl.ds(0, experts - 1)
        pltpu.make_async_copy(source.at[peers], target.at[peers], a2a_send_sem.at[phase]).wait()

    for n in (0, 3, 8, 9):
        loads[n].wait()
    cell = expert_ref[...] * cap + slot_ref[...]
    pick = (lax.broadcasted_iota(jnp.int32, (cells, samples), 0) == cell).astype(BF16)
    rows = matmul(pick, in_ref[...], ((1,), (0,)))
    row_send[...] = rows.reshape(experts, cap, width).astype(BF16)
    head_rows[...] = jnp.zeros_like(head_rows)
    for h in range(4):
        head_rows[h * cap : (h + 1) * cap, :] = jnp.broadcast_to(
            hw_ref[h : h + 1, :].astype(F32), (cap, width)
        )
    pl.semaphore_wait(barrier, experts + replicas - 2)
    exchange(0, row_send, row_recv)
    arrive(0, row_send, row_recv)
    acts[0] = row_recv[...].astype(F32).reshape(cells, width).astype(BF16)

    for n in (1, 2, 4, 5, 6, 7, 10):
        loads[n].wait()

    def forward(layer, c):
        v = matmul(acts[layer], w_ref[layer], ((1,), (0,))) + b_ref[pl.ds(layer, 1), :]
        acts[layer + 1] = softplus(v).astype(BF16)
        return c

    lax.fori_loop(0, layers - 1, forward, 0)
    features = (
        matmul(acts[layers - 1], w_ref[layers - 1], ((1,), (0,))) + b_ref[layers - 1 : layers, :]
    ).astype(BF16)
    acts[layers] = features

    own_slot = lax.broadcasted_iota(jnp.int32, (cells, lanes), 0) % cap == (
        lax.broadcasted_iota(jnp.int32, (cells, lanes), 1) % cap
    )
    product = matmul(features, head_rows[...].astype(BF16), ((1,), (1,)))
    up_send[...] = (
        jnp.where(own_slot, product, 0.0).reshape(experts, cap, lanes).sum(axis=1, keepdims=True)
    )
    exchange(1, up_send, up_recv)
    arrive(1, up_send, up_recv)

    named = (lax.broadcasted_iota(jnp.int32, (experts, samples), 0) == expert_ref[...]).astype(F32)
    table = up_recv[...].reshape(experts, lanes)
    picked = matmul(table, named, ((0,), (0,)), HIGHEST)
    slot_hot = lax.broadcasted_iota(jnp.int32, (cap, samples), 0) == slot_ref[...]
    unscaled = jnp.concatenate(
        [
            jnp.where(slot_hot, picked[h * cap : (h + 1) * cap, :], 0.0).sum(axis=0, keepdims=True)
            for h in range(4)
        ],
        axis=0,
    )
    gate = gate_ref[...]
    grad_logits = composite(unscaled, gate, hb_ref, spacing_ref[...], ray_ref[...], ct_ref)
    placed = jnp.concatenate(
        [
            jnp.where(slot_hot, jnp.broadcast_to(gate * grad_logits[h], (cap, samples)), 0.0)
            for h in range(4)
        ]
        + [jnp.zeros((lanes - 4 * cap, samples), F32)],
        axis=0,
    )
    down_send[...] = matmul(named, placed, ((1,), (1,)), HIGHEST).reshape(experts, 1, lanes)
    exchange(2, down_send, down_recv)
    for h in range(4):
        head_part[4 + h : 5 + h, :] = jnp.broadcast_to(
            grad_logits[h].sum(axis=1, keepdims=True), (1, width)
        )
    arrive(2, down_send, down_recv)

    coming = jnp.where(
        own_slot,
        jnp.broadcast_to(down_recv[...], (experts, cap, lanes)).reshape(cells, lanes),
        0.0,
    )
    first_upstream = matmul(coming, head_rows[...], ((1,), (0,)), HIGHEST).astype(BF16)
    head_all = matmul(coming, acts[layers].astype(F32), ((0,), (0,)), HIGHEST)
    for h in range(4):
        head_part[h : h + 1, :] = head_all[h * cap : (h + 1) * cap, :].sum(axis=0, keepdims=True)
    acts[layers] = first_upstream

    def head_peer(stage, k):
        extent, stride = stages[stage]
        mine = lax.rem(me_e // stride, extent)
        return mine, me_e + (lax.rem(mine + k, extent) - mine) * stride

    def head_start(stage):
        extent, stride = stages[stage]
        mine, _ = head_peer(stage, 0)
        head_recv[stage, mine] = head_part[...]
        for k in range(1, extent):
            pltpu.make_async_remote_copy(
                src_ref=head_part,
                dst_ref=head_recv.at[stage, mine],
                send_sem=head_send_sem.at[stage],
                recv_sem=head_recv_sem.at[stage],
                device_id={"expert": head_peer(stage, k)[1]},
                device_id_type=MESH,
            ).start()

    def head_finish(stage):
        extent, stride = stages[stage]
        block = head_recv.at[stage, pl.ds(0, extent - 1)]
        pltpu.make_async_copy(block, block, head_recv_sem.at[stage]).wait()
        pltpu.make_async_copy(block, block, head_send_sem.at[stage]).wait()
        total = head_recv[stage, 0]
        for k in range(1, extent):
            total = total + head_recv[stage, k]
        head_part[...] = total

    def chain_copy(way, layer, step):
        return pltpu.make_async_remote_copy(
            src_ref=chain_send.at[way, step * layers + layer],
            dst_ref=chain_recv.at[way, step, layer],
            send_sem=chain_send_sem.at[way],
            recv_sem=chain_recv_sem.at[way, step, layer],
            device_id={"dp": below if way == 0 else above},
            device_id_type=MESH,
        )

    def shard_of(way, distance):
        if way == 0:
            return lax.rem(me_d + replicas - distance, replicas)
        return lax.rem(me_d + distance, replicas)

    def weight_grad(layer):
        upstream = acts[layers]
        part[layer] = matmul(acts[layer], upstream, ((0,), (0,))).reshape(replicas, piece, width)
        small[lax.rem(layer, replicas), pl.ds(layer // replicas, 1), :] = upstream.astype(F32).sum(
            axis=0, keepdims=True
        )
        for way in range(2):
            chain_send[way, layer] = part[layer, shard_of(way, reach(way, layer))].astype(BF16)
            chain_copy(way, layer, 0).start()

    def hop(step, layer, way):
        chain_copy(way, layer, step - 1).wait_recv()
        chain_send[way, step * layers + layer] = (
            chain_recv[way, step - 1, layer].astype(F32)
            + part[layer, shard_of(way, reach(way, layer) - step)]
        ).astype(BF16)
        chain_copy(way, layer, step).start()

    lag = 3

    def hops(i, count):
        for step in range(1, most - 1):
            if step <= count:
                for way in range(2):
                    pass

    def backward_with(count):
        def backward(i, c):
            layer = layers - 1 - i
            weight_grad(layer)
            hops(i, count)
            spread = matmul(acts[layers], w_ref[layer], ((1,), (1,)))
            acts[layers] = (spread * one_minus_exp(acts[layer].astype(F32))).astype(BF16)
            return c

        return backward

    marks = [lag, 2 * lag, layers - 1]
    head_start(0)
    done = 0
    for stage in range(3):
        lax.fori_loop(done, marks[stage], backward_with(stage), 0)
        done = marks[stage]
        if stage < len(stages) and stage < 2:
            head_finish(stage)
            if stage + 1 < len(stages):
                head_start(stage + 1)
    spread = matmul(acts[layers], w_ref[0], ((1,), (1,)))
    back_send[...] = spread.reshape(experts, cap, width).astype(BF16)
    back_recv[me_e] = back_send[me_e]
    weight_grad(0)
    hops(layers - 1, 2)

    work = sum(layers for step in range(1, most - 1)) + layers
    per_slot = pl.cdiv(experts - 1, work)

    def feed(slot):
        for n in range(per_slot):
            k = 1 + slot * per_slot + n

            @pl.when(k < experts)
            def _():
                exchange_one(3, back_send, back_recv, k)

    def by_pairs(step_of, first_slot=None):
        def pair(i, c):
            for odd in (1, 0):
                step_of(layers - 2 - 2 * i + odd, odd)
            if first_slot is not None:
                feed(first_slot + i)
            return c

        lax.fori_loop(0, layers // 2, pair, 0)

    slot = 0
    for step in range(1, most - 1):

        def remaining(i, c):
            for way in range(2):
                hop(step, layers - 1 - i, way)
            feed(slot + i)
            return c

        begin = 0
        lax.fori_loop(begin, layers, remaining, 0)
        slot += layers - begin

    def last_hop(layer, odd):
        for way in range(2):
            if most - 1 < reach(way, odd):
                hop(most - 1, layer, way)

    if len(stages) > 2:
        head_finish(2)
    for row in range(8):
        place = layers + row
        small[place % replicas, place // replicas : place // replicas + 1, :] = head_part[
            row : row + 1, :
        ]
    small_recv[me_d] = small[me_d]

    def small_start(k, c):
        peer = lax.rem(me_d + k, replicas)
        pltpu.make_async_remote_copy(
            src_ref=small.at[peer],
            dst_ref=small_recv.at[me_d],
            send_sem=small_send_sem.at[0],
            recv_sem=small_recv_sem.at[0],
            device_id={"dp": peer},
            device_id_type=MESH,
        ).start()
        return c

    lax.fori_loop(1, replicas, small_start, 0)

    if most > 1:
        by_pairs(last_hop, slot)
        slot += layers // 2

    def ring_copy(way, layer, step):
        owner = shard_of(1 - way, step)
        return pltpu.make_async_remote_copy(
            src_ref=out_w.at[owner, layer],
            dst_ref=out_w.at[owner, layer],
            send_sem=ring_send_sem.at[way],
            recv_sem=ring_recv_sem.at[way, step, layer],
            device_id={"dp": below if way == 0 else above},
            device_id_type=MESH,
        )

    def ring_arrive(way, layer, step):
        owner = shard_of(1 - way, step + 1)
        pltpu.make_async_copy(
            out_w.at[owner, layer], out_w.at[owner, layer], ring_recv_sem.at[way, step, layer]
        ).wait()

    def finish(layer, odd):
        total = part[layer, me_d]
        for way in range(2):
            chain_copy(way, layer, reach(way, odd) - 1).wait_recv()
            total = total + chain_recv[way, reach(way, odd) - 1, layer].astype(F32)
        out_w[me_d, layer] = total.astype(BF16)
        for way in range(2):
            ring_copy(way, layer, 0).start()

    by_pairs(finish, slot)

    peers_d = small_recv.at[pl.ds(0, replicas - 1)]
    pltpu.make_async_copy(peers_d, peers_d, small_recv_sem.at[0]).wait()
    total = small_recv[0]
    for k in range(1, replicas):
        total = total + small_recv[k]
    out_small[me_d] = total

    def small_spread(k, c):
        pltpu.make_async_remote_copy(
            src_ref=out_small.at[me_d],
            dst_ref=out_small.at[me_d],
            send_sem=small_send_sem.at[1],
            recv_sem=small_recv_sem.at[1],
            device_id={"dp": lax.rem(me_d + k, replicas)},
            device_id_type=MESH,
        ).start()
        return c

    lax.fori_loop(1, replicas, small_spread, 0)

    for step in range(1, most):

        def forward_on(layer, odd):
            for way in range(2):
                if step < reach(way, odd):
                    ring_arrive(way, layer, step - 1)
                    ring_copy(way, layer, step).start()

        by_pairs(forward_on)

    arrive(3, back_send, back_recv)
    slots = back_recv[...].astype(F32).reshape(cells, width).astype(BF16)
    again = (lax.broadcasted_iota(jnp.int32, (cells, samples), 0) == cell).astype(BF16)
    out_in[...] = matmul(again, slots, ((0,), (0,))).astype(BF16)

    pltpu.make_async_copy(peers_d, peers_d, small_recv_sem.at[1]).wait()

    def last(layer, odd):
        for way in range(2):
            ring_arrive(way, layer, reach(way, odd) - 1)

    by_pairs(last)

    sent(0, row_send, row_recv)
    sent(1, up_send, up_recv)
    sent(2, down_send, down_recv)
    sent(3, back_send, back_recv)
    for n in range(2):
        pltpu.make_async_copy(peers_d, peers_d, small_send_sem.at[n]).wait()
    for way in range(2):
        gone = chain_send.at[way, pl.ds(0, most * layers - layers // 2)]
        pltpu.make_async_copy(gone, gone, chain_send_sem.at[way]).wait()
        pltpu.make_async_copy(gone, gone, ring_send_sem.at[way]).wait()


def write_out(
    in_ref, w_ref, small_ref, out_in, out_w, out_b, out_hw, out_hb, wide, out_sem
):
    layers = wide.shape[0]
    stores = [
        pltpu.make_async_copy(wide.at[n], out_w.at[n], out_sem.at[n]) for n in range(layers)
    ]
    for n in range(layers):
        wide[n] = w_ref[:, n].astype(F32)
        stores[n].start()
    out_in[...] = in_ref[...]
    replicas = small_ref.shape[0]

    def row(place):
        return small_ref[place % replicas, place // replicas : place // replicas + 1, :]

    for n in range(layers):
        out_b[n : n + 1, :] = row(n)
    for h in range(4):
        out_hw[h : h + 1, :] = row(layers + h)
        out_hb[0:1, h : h + 1] = row(layers + 4 + h)[:, 0:1]
    for store in stores:
        store.wait()


def per_device(
    replicas,
    experts,
    inputs,
    layer_weights,
    layer_biases,
    head_weight,
    head_bias,
    gate_values,
    spacing,
    ray_index,
    expert_index,
    slot_index,
    color_cotangent,
):
    samples, width = inputs.shape[2:]
    layers = layer_weights.shape[1]
    cap = 2 * samples // experts
    cells = experts * cap
    piece = width // replicas
    steps = replicas // 2
    lanes = 128
    dma = pltpu.SemaphoreType.DMA
    operands = (
        inputs.reshape(samples, width),
        layer_weights[0],
        layer_biases[0],
        head_weight,
        head_bias.reshape(1, 4),
        gate_values.reshape(1, samples),
        spacing.reshape(1, samples),
        ray_index.reshape(1, samples),
        expert_index.reshape(1, samples),
        slot_index.reshape(1, samples),
        color_cotangent.reshape(3, 1, color_cotangent.shape[3]),
    )
    whole = pl.BlockSpec(memory_space=pltpu.VMEM)
    out_in, out_w, out_small = pl.pallas_call(
        functools.partial(body, replicas, experts),
        out_shape=(
            jax.ShapeDtypeStruct((samples, width), BF16),
            jax.ShapeDtypeStruct((replicas, layers, piece, width), BF16),
            jax.ShapeDtypeStruct((replicas, (layers + 8) // replicas, width), F32),
        ),
        in_specs=[pl.BlockSpec(memory_space=pltpu.HBM)] * 11,
        out_specs=(whole,) * 3,
        scratch_shapes=[
            *(pltpu.VMEM(a.shape, a.dtype) for a in operands),
            dma((11,)),
            pltpu.VMEM((layers + 1, cells, width), BF16),
            pltpu.VMEM((lanes, width), F32),
            pltpu.VMEM((experts, cap, width), BF16),
            pltpu.VMEM((experts, cap, width), BF16),
            pltpu.VMEM((experts, 1, lanes), F32),
            pltpu.VMEM((experts, 1, lanes), F32),
            pltpu.VMEM((experts, 1, lanes), F32),
            pltpu.VMEM((experts, 1, lanes), F32),
            pltpu.VMEM((experts, cap, width), BF16),
            pltpu.VMEM((experts, cap, width), BF16),
            pltpu.VMEM((layers, replicas, piece, width), F32),
            pltpu.VMEM((2, steps * layers, piece, width), BF16),
            pltpu.VMEM((2, steps, layers, piece, width), BF16),
            pltpu.VMEM((8, width), F32),
            pltpu.VMEM((3, 8, 8, width), F32),
            pltpu.VMEM((replicas, (layers + 8) // replicas, width), F32),
            pltpu.VMEM((replicas, (layers + 8) // replicas, width), F32),
            dma((4,)),
            dma((4,)),
            dma((2,)),
            dma((2, steps, layers)),
            dma((2,)),
            dma((2, steps, layers)),
            dma((3,)),
            dma((3,)),
            dma((2,)),
            dma((2,)),
        ],
        compiler_params=pltpu.CompilerParams(
            collective_id=0, has_side_effects=True, vmem_limit_bytes=32 * 1024 * 1024
        ),
    )(*(pltpu.with_memory_space_constraint(a, pltpu.HBM) for a in operands))
    grad_inputs, grad_weights, grad_biases, grad_head_weight, grad_head_bias = pl.pallas_call(
        write_out,
        out_shape=(
            jax.ShapeDtypeStruct((samples, width), BF16),
            jax.ShapeDtypeStruct((layers, replicas, piece, width), F32),
            jax.ShapeDtypeStruct((layers, width), F32),
            jax.ShapeDtypeStruct((4, width), F32),
            jax.ShapeDtypeStruct((1, 4), F32),
        ),
        in_specs=[whole] * 3,
        out_specs=(whole, pl.BlockSpec(memory_space=pl.ANY), whole, whole, whole),
        scratch_shapes=[
            pltpu.VMEM((layers, replicas, piece, width), F32),
            dma((layers,)),
        ],
        compiler_params=pltpu.CompilerParams(vmem_limit_bytes=16 * 1024 * 1024),
    )(out_in, out_w, out_small)
    return (
        grad_inputs.reshape(1, 1, samples, width),
        grad_weights.reshape(1, layers, width, width),
        grad_biases[None],
        grad_head_weight,
        grad_head_bias.reshape(4),
    )


def solution(mesh):
    in_specs = (
        P("dp", "expert", None, None),
        P("expert", None, None, None),
        P("expert", None, None),
        P(),
        P(),
        P("dp", "expert", None),
        P("dp", "expert", None),
        P("dp", "expert", None),
        P("dp", "expert", None),
        P("dp", "expert", None),
        P("dp", "expert", None, None),
    )
    out_specs = (
        P("dp", "expert", None, None),
        P("expert", None, None, None),
        P("expert", None, None),
        P(),
        P(),
    )
    return jax.shard_map(
        functools.partial(per_device, mesh.shape["dp"], mesh.shape["expert"]),
        mesh=mesh,
        in_specs=in_specs,
        out_specs=out_specs,
        check_vma=False,
    )
```

```python
import functools

import jax
import jax.numpy as jnp
from jax import lax
from jax.experimental import pallas as pl
from jax.experimental.pallas import tpu as pltpu
from jax.sharding import PartitionSpec as P

MESH = pl.DeviceIdType.MESH
HIGHEST = lax.Precision.HIGHEST
F32 = jnp.float32
BF16 = jnp.bfloat16


def matmul(a, b, dims, precision=None):
    return lax.dot_general(
        a, b, (dims, ((), ())), precision=precision, preferred_element_type=F32
    )


def softplus(v):
    return jnp.maximum(v, 0.0) + jnp.log1p(jnp.exp(-jnp.abs(v)))


def sigmoid(v):
    small = jnp.exp(-jnp.abs(v))
    return jnp.where(v >= 0.0, 1.0, small) / (1.0 + small)


def one_minus_exp(t):
    series = t * (1.0 - t * (0.5 - t * (1.0 / 6.0 - t * (1.0 / 24.0 - t * (1.0 / 120.0)))))
    return jnp.where(t < 0.06, series, 1.0 - jnp.exp(-t))


def factors(experts):
    stages = []
    stride = 1
    for extent in (2, 4, 8):
        extent = min(extent, experts // stride)
        if extent > 1:
            stages.append((extent, stride))
            stride *= extent
    return stages


def composite(unscaled, gate, hb_ref, spacing, ray, ct_ref):
    rays = ct_ref.shape[2]
    samples = ray.shape[1]
    logits = [gate * unscaled[h : h + 1, :] + hb_ref[0:1, h : h + 1] for h in range(4)]
    sigma = softplus(logits[0])
    colors = [sigmoid(logits[h]) for h in range(1, 4)]
    tau = sigma * spacing
    hot = (lax.broadcasted_iota(jnp.int32, (8, samples), 0) == ray).astype(F32)
    same = matmul(hot.astype(BF16), hot.astype(BF16), ((0,), (0,)))
    before = lax.broadcasted_iota(jnp.int32, (samples, samples), 0)
    after = lax.broadcasted_iota(jnp.int32, (samples, samples), 1)
    earlier = jnp.where(before < after, same, 0.0)
    inside = matmul(jnp.broadcast_to(tau, (8, samples)), earlier, ((1,), (0,)), HIGHEST)[0:1, :]
    clear = jnp.exp(-inside)
    opacity = one_minus_exp(tau)
    weight = clear * opacity
    grads = []
    weight_grad = jnp.zeros_like(weight)
    for k in range(3):
        cotangent = jnp.zeros_like(weight)
        for r in range(rays):
            cotangent += ct_ref[k, 0:1, r : r + 1] * hot[r : r + 1, :]
        weight_grad += cotangent * colors[k]
        grads.append(cotangent * weight * colors[k] * (1.0 - colors[k]))
    inside_grad = -weight_grad * weight
    spread = matmul(
        jnp.broadcast_to(inside_grad, (8, samples)), earlier, ((1,), (1,)), HIGHEST
    )[0:1, :]
    tau_grad = weight_grad * clear * jnp.exp(-tau) + spread
    first = tau_grad * spacing * sigmoid(logits[0])
    return [first] + grads


def body(
    replicas,
    experts,
    *refs,
):
    sources, refs = refs[:11], refs[11:]
    (out_in, out_w, out_small), refs = refs[:3], refs[3:]
    loaded, (load_sem, *refs) = refs[:11], refs[11:]
    loads = [pltpu.make_async_copy(a, b, load_sem.at[n]) for n, (a, b) in enumerate(zip(sources, loaded))]
    for load in loads:
        load.start()
    compute(replicas, experts, loads, *loaded, out_in, out_w, out_small, *refs)


def compute(
    replicas,
    experts,
    loads,
    in_ref,
    w_ref,
    b_ref,
    hw_ref,
    hb_ref,
    gate_ref,
    spacing_ref,
    ray_ref,
    expert_ref,
    slot_ref,
    ct_ref,
    out_in,
    out_w,
    out_small,
    acts,
    head_rows,
    row_send,
    row_recv,
    up_send,
    up_recv,
    down_send,
    down_recv,
    back_send,
    back_recv,
    part,
    chain_send,
    chain_recv,
    extra_send,
    extra_recv,
    head_part,
    head_recv,
    small,
    small_recv,
    a2a_send_sem,
    a2a_recv_sem,
    chain_send_sem,
    chain_recv_sem,
    extra_send_sem,
    extra_recv_sem,
    ring_send_sem,
    ring_recv_sem,
    head_send_sem,
    head_recv_sem,
    small_send_sem,
    small_recv_sem,
):
    samples, width = in_ref.shape
    layers = w_ref.shape[0]
    cap = 2 * samples // experts
    cells = experts * cap
    lanes = head_rows.shape[0]
    piece = width // replicas
    me_d = lax.axis_index("dp")
    me_e = lax.axis_index("expert")
    above = lax.rem(me_d + 1, replicas)
    below = lax.rem(me_d + replicas - 1, replicas)
    most = replicas // 2

    length = most - 1

    def beyond(layer):
        return lax.rem(me_d + replicas - 2 + 4 * (layer % 2), replicas)

    stages = factors(experts)

    barrier = pltpu.get_barrier_semaphore()

    def greet_e(k, c):
        pl.semaphore_signal(
            barrier, inc=1, device_id={"expert": lax.rem(me_e + k, experts)}, device_id_type=MESH
        )
        return c

    def greet_d(k, c):
        pl.semaphore_signal(
            barrier, inc=1, device_id={"dp": lax.rem(me_d + k, replicas)}, device_id_type=MESH
        )
        return c

    lax.fori_loop(1, experts, greet_e, 0)
    lax.fori_loop(1, replicas, greet_d, 0)

    def exchange(phase, source, target):
        def send(k, c):
            exchange_one(phase, source, target, k)
            return c

        lax.fori_loop(1, experts, send, 0)
        target[me_e] = source[me_e]

    def exchange_one(phase, source, target, k):
        ahead = experts // 2 - k // 2
        peer = lax.rem(me_e + experts + ahead * (1 - 2 * (k % 2)), experts)
        pltpu.make_async_remote_copy(
            src_ref=source.at[peer],
            dst_ref=target.at[me_e],
            send_sem=a2a_send_sem.at[phase],
            recv_sem=a2a_recv_sem.at[phase],
            device_id={"expert": peer},
            device_id_type=MESH,
        ).start()

    def arrive(phase, source, target):
        peers = pl.ds(0, experts - 1)
        pltpu.make_async_copy(source.at[peers], target.at[peers], a2a_recv_sem.at[phase]).wait()

    def sent(phase, source, target):
        peers = pl.ds(0, experts - 1)
        pltpu.make_async_copy(source.at[peers], target.at[peers], a2a_send_sem.at[phase]).wait()

    for n in (0, 3, 8, 9):
        loads[n].wait()
    cell = expert_ref[...] * cap + slot_ref[...]
    pick = (lax.broadcasted_iota(jnp.int32, (cells, samples), 0) == cell).astype(BF16)
    rows = matmul(pick, in_ref[...], ((1,), (0,)))
    row_send[...] = rows.reshape(experts, cap, width).astype(BF16)
    head_rows[...] = jnp.zeros_like(head_rows)
    for h in range(4):
        head_rows[h * cap : (h + 1) * cap, :] = jnp.broadcast_to(
            hw_ref[h : h + 1, :].astype(F32), (cap, width)
        )
    pl.semaphore_wait(barrier, experts + replicas - 2)
    exchange(0, row_send, row_recv)
    arrive(0, row_send, row_recv)
    acts[0] = row_recv[...].astype(F32).reshape(cells, width).astype(BF16)

    for n in (1, 2, 4, 5, 6, 7, 10):
        loads[n].wait()

    def forward(layer, c):
        v = matmul(acts[layer], w_ref[layer], ((1,), (0,))) + b_ref[pl.ds(layer, 1), :]
        acts[layer + 1] = softplus(v).astype(BF16)
        return c

    lax.fori_loop(0, layers - 1, forward, 0)
    features = (
        matmul(acts[layers - 1], w_ref[layers - 1], ((1,), (0,))) + b_ref[layers - 1 : layers, :]
    ).astype(BF16)
    acts[layers] = features

    own_slot = lax.broadcasted_iota(jnp.int32, (cells, lanes), 0) % cap == (
        lax.broadcasted_iota(jnp.int32, (cells, lanes), 1) % cap
    )
    product = matmul(features, head_rows[...].astype(BF16), ((1,), (1,)))
    up_send[...] = (
        jnp.where(own_slot, product, 0.0).reshape(experts, cap, lanes).sum(axis=1, keepdims=True)
    )
    exchange(1, up_send, up_recv)
    arrive(1, up_send, up_recv)

    named = (lax.broadcasted_iota(jnp.int32, (experts, samples), 0) == expert_ref[...]).astype(F32)
    table = up_recv[...].reshape(experts, lanes)
    picked = matmul(table, named, ((0,), (0,)), HIGHEST)
    slot_hot = lax.broadcasted_iota(jnp.int32, (cap, samples), 0) == slot_ref[...]
    unscaled = jnp.concatenate(
        [
            jnp.where(slot_hot, picked[h * cap : (h + 1) * cap, :], 0.0).sum(axis=0, keepdims=True)
            for h in range(4)
        ],
        axis=0,
    )
    gate = gate_ref[...]
    grad_logits = composite(unscaled, gate, hb_ref, spacing_ref[...], ray_ref[...], ct_ref)
    placed = jnp.concatenate(
        [
            jnp.where(slot_hot, jnp.broadcast_to(gate * grad_logits[h], (cap, samples)), 0.0)
            for h in range(4)
        ]
        + [jnp.zeros((lanes - 4 * cap, samples), F32)],
        axis=0,
    )
    down_send[...] = matmul(named, placed, ((1,), (1,)), HIGHEST).reshape(experts, 1, lanes)
    exchange(2, down_send, down_recv)
    for h in range(4):
        head_part[4 + h : 5 + h, :] = jnp.broadcast_to(
            grad_logits[h].sum(axis=1, keepdims=True), (1, width)
        )
    arrive(2, down_send, down_recv)

    coming = jnp.where(
        own_slot,
        jnp.broadcast_to(down_recv[...], (experts, cap, lanes)).reshape(cells, lanes),
        0.0,
    )
    first_upstream = matmul(coming, head_rows[...], ((1,), (0,)), HIGHEST).astype(BF16)
    head_all = matmul(coming, acts[layers].astype(F32), ((0,), (0,)), HIGHEST)
    for h in range(4):
        head_part[h : h + 1, :] = head_all[h * cap : (h + 1) * cap, :].sum(axis=0, keepdims=True)
    acts[layers] = first_upstream

    def head_peer(stage, k):
        extent, stride = stages[stage]
        mine = lax.rem(me_e // stride, extent)
        return mine, me_e + (lax.rem(mine + k, extent) - mine) * stride

    def head_start(stage):
        extent, stride = stages[stage]
        mine, _ = head_peer(stage, 0)
        head_recv[stage, mine] = head_part[...]
        for k in range(1, extent):
            pltpu.make_async_remote_copy(
                src_ref=head_part,
                dst_ref=head_recv.at[stage, mine],
                send_sem=head_send_sem.at[stage],
                recv_sem=head_recv_sem.at[stage],
                device_id={"expert": head_peer(stage, k)[1]},
                device_id_type=MESH,
            ).start()

    def head_finish(stage):
        extent, stride = stages[stage]
        block = head_recv.at[stage, pl.ds(0, extent - 1)]
        pltpu.make_async_copy(block, block, head_recv_sem.at[stage]).wait()
        pltpu.make_async_copy(block, block, head_send_sem.at[stage]).wait()
        total = head_recv[stage, 0]
        for k in range(1, extent):
            total = total + head_recv[stage, k]
        head_part[...] = total

    def chain_copy(way, layer, step):
        return pltpu.make_async_remote_copy(
            src_ref=chain_send.at[way, step * layers + layer],
            dst_ref=chain_recv.at[way, step, layer],
            send_sem=chain_send_sem.at[way],
            recv_sem=chain_recv_sem.at[way, step, layer],
            device_id={"dp": below if way == 0 else above},
            device_id_type=MESH,
        )

    def extra_copy(layer):
        return pltpu.make_async_remote_copy(
            src_ref=extra_send.at[layer],
            dst_ref=extra_recv.at[layer],
            send_sem=extra_send_sem.at[0],
            recv_sem=extra_recv_sem.at[0, layer],
            device_id={"dp": beyond(layer)},
            device_id_type=MESH,
        )

    def shard_of(way, distance):
        if way == 0:
            return lax.rem(me_d + replicas - distance, replicas)
        return lax.rem(me_d + distance, replicas)

    def weight_grad(layer):
        upstream = acts[layers]
        part[layer] = matmul(acts[layer], upstream, ((0,), (0,))).reshape(replicas, piece, width)
        small[lax.rem(layer, replicas), pl.ds(layer // replicas, 1), :] = upstream.astype(F32).sum(
            axis=0, keepdims=True
        )
        extra_send[layer] = part[layer, lax.rem(me_d + most, replicas)].astype(BF16)
        extra_copy(layer).start()
        for way in range(2):
            chain_send[way, layer] = part[layer, shard_of(way, length)].astype(BF16)
            chain_copy(way, layer, 0).start()

    def hop(step, layer, way, odd):
        chain_copy(way, layer, step - 1).wait_recv()
        total = (
            chain_recv[way, step - 1, layer].astype(F32)
            + part[layer, shard_of(way, length - step)]
        )
        if step == 1 and way == odd:
            extra_copy(layer).wait_recv()
            total = total + extra_recv[layer].astype(F32)
        chain_send[way, step * layers + layer] = total.astype(BF16)
        chain_copy(way, layer, step).start()

    lag = 3

    def backward_with(count):
        def backward(i, c):
            layer = layers - 1 - i
            weight_grad(layer)
            spread = matmul(acts[layers], w_ref[layer], ((1,), (1,)))
            acts[layers] = (spread * one_minus_exp(acts[layer].astype(F32))).astype(BF16)
            return c

        return backward

    marks = [lag, 2 * lag, layers - 1]
    head_start(0)
    done = 0
    for stage in range(3):
        lax.fori_loop(done, marks[stage], backward_with(stage), 0)
        done = marks[stage]
        if stage < len(stages) and stage < 2:
            head_finish(stage)
            if stage + 1 < len(stages):
                head_start(stage + 1)
    spread = matmul(acts[layers], w_ref[0], ((1,), (1,)))
    back_send[...] = spread.reshape(experts, cap, width).astype(BF16)
    back_recv[me_e] = back_send[me_e]
    weight_grad(0)

    work = length * layers // 2
    per_slot = pl.cdiv(experts - 1, work)

    def feed(slot):
        for n in range(per_slot):
            k = 1 + slot * per_slot + n

            @pl.when(k < experts)
            def _():
                exchange_one(3, back_send, back_recv, k)

    def by_pairs(step_of, first_slot=None):
        def pair(i, c):
            for odd in (1, 0):
                step_of(layers - 2 - 2 * i + odd, odd)
            if first_slot is not None:
                feed(first_slot + i)
            return c

        lax.fori_loop(0, layers // 2, pair, 0)

    slot = 0
    for step in range(1, length):

        def each(layer, odd):
            for way in range(2):
                hop(step, layer, way, odd)

        by_pairs(each, slot)
        slot += layers // 2

    if len(stages) > 2:
        head_finish(2)
    for row in range(8):
        place = layers + row
        small[place % replicas, place // replicas : place // replicas + 1, :] = head_part[
            row : row + 1, :
        ]
    small_recv[me_d] = small[me_d]

    def small_start(k, c):
        peer = lax.rem(me_d + k, replicas)
        pltpu.make_async_remote_copy(
            src_ref=small.at[peer],
            dst_ref=small_recv.at[me_d],
            send_sem=small_send_sem.at[0],
            recv_sem=small_recv_sem.at[0],
            device_id={"dp": peer},
            device_id_type=MESH,
        ).start()
        return c

    lax.fori_loop(1, replicas, small_start, 0)


    def ring_copy(way, layer, step):
        owner = shard_of(1 - way, step)
        return pltpu.make_async_remote_copy(
            src_ref=out_w.at[owner, layer],
            dst_ref=out_w.at[owner, layer],
            send_sem=ring_send_sem.at[way],
            recv_sem=ring_recv_sem.at[way, step, layer],
            device_id={"dp": below if way == 0 else above},
            device_id_type=MESH,
        )

    def extra_ring(layer):
        owner = lax.rem(me_d + replicas + 2 - 4 * (layer % 2), replicas)
        return pltpu.make_async_remote_copy(
            src_ref=out_w.at[owner, layer],
            dst_ref=out_w.at[owner, layer],
            send_sem=extra_send_sem.at[1],
            recv_sem=extra_recv_sem.at[1, layer],
            device_id={"dp": beyond(layer)},
            device_id_type=MESH,
        )

    def ring_arrive(way, layer, step):
        owner = shard_of(1 - way, step + 1)
        pltpu.make_async_copy(
            out_w.at[owner, layer], out_w.at[owner, layer], ring_recv_sem.at[way, step, layer]
        ).wait()

    def finish(layer, odd):
        total = part[layer, me_d]
        for way in range(2):
            chain_copy(way, layer, length - 1).wait_recv()
            total = total + chain_recv[way, length - 1, layer].astype(F32)
        out_w[me_d, layer] = total.astype(BF16)
        for way in range(2):
            ring_copy(way, layer, 0).start()

    by_pairs(finish, slot)

    peers_d = small_recv.at[pl.ds(0, replicas - 1)]
    pltpu.make_async_copy(peers_d, peers_d, small_recv_sem.at[0]).wait()
    total = small_recv[0]
    for k in range(1, replicas):
        total = total + small_recv[k]
    out_small[me_d] = total

    def small_spread(k, c):
        pltpu.make_async_remote_copy(
            src_ref=out_small.at[me_d],
            dst_ref=out_small.at[me_d],
            send_sem=small_send_sem.at[1],
            recv_sem=small_recv_sem.at[1],
            device_id={"dp": lax.rem(me_d + k, replicas)},
            device_id_type=MESH,
        ).start()
        return c

    lax.fori_loop(1, replicas, small_spread, 0)

    for step in range(1, length):

        def forward_on(layer, odd):
            for way in range(2):
                ring_arrive(way, layer, step - 1)
                ring_copy(way, layer, step).start()
                if step == length - 1 and way == odd:
                    extra_ring(layer).start()

        by_pairs(forward_on)

    arrive(3, back_send, back_recv)
    slots = back_recv[...].astype(F32).reshape(cells, width).astype(BF16)
    again = (lax.broadcasted_iota(jnp.int32, (cells, samples), 0) == cell).astype(BF16)
    out_in[...] = matmul(again, slots, ((0,), (0,))).astype(BF16)

    pltpu.make_async_copy(peers_d, peers_d, small_recv_sem.at[1]).wait()

    def last(layer, odd):
        for way in range(2):
            ring_arrive(way, layer, length - 1)
        owner = lax.rem(me_d + most, replicas)
        pltpu.make_async_copy(
            out_w.at[owner, layer], out_w.at[owner, layer], extra_recv_sem.at[1, layer]
        ).wait()

    by_pairs(last)

    sent(0, row_send, row_recv)
    sent(1, up_send, up_recv)
    sent(2, down_send, down_recv)
    sent(3, back_send, back_recv)
    for n in range(2):
        pltpu.make_async_copy(peers_d, peers_d, small_send_sem.at[n]).wait()
    for way in range(2):
        pltpu.make_async_copy(extra_send, extra_send, extra_send_sem.at[way]).wait()
        gone = chain_send.at[way, pl.ds(0, length * layers)]
        pltpu.make_async_copy(gone, gone, chain_send_sem.at[way]).wait()
        pltpu.make_async_copy(gone, gone, ring_send_sem.at[way]).wait()


def write_out(
    in_ref, w_ref, small_ref, out_in, out_w, out_b, out_hw, out_hb, wide, out_sem
):
    layers = wide.shape[0]
    stores = [
        pltpu.make_async_copy(wide.at[n], out_w.at[n], out_sem.at[n]) for n in range(layers)
    ]
    for n in range(layers):
        wide[n] = w_ref[:, n].astype(F32)
        stores[n].start()
    out_in[...] = in_ref[...]
    replicas = small_ref.shape[0]

    def row(place):
        return small_ref[place % replicas, place // replicas : place // replicas + 1, :]

    for n in range(layers):
        out_b[n : n + 1, :] = row(n)
    for h in range(4):
        out_hw[h : h + 1, :] = row(layers + h)
        out_hb[0:1, h : h + 1] = row(layers + 4 + h)[:, 0:1]
    for store in stores:
        store.wait()


def per_device(
    replicas,
    experts,
    inputs,
    layer_weights,
    layer_biases,
    head_weight,
    head_bias,
    gate_values,
    spacing,
    ray_index,
    expert_index,
    slot_index,
    color_cotangent,
):
    samples, width = inputs.shape[2:]
    layers = layer_weights.shape[1]
    cap = 2 * samples // experts
    cells = experts * cap
    piece = width // replicas
    steps = replicas // 2 - 1
    assert replicas == 8
    lanes = 128
    dma = pltpu.SemaphoreType.DMA
    operands = (
        inputs.reshape(samples, width),
        layer_weights[0],
        layer_biases[0],
        head_weight,
        head_bias.reshape(1, 4),
        gate_values.reshape(1, samples),
        spacing.reshape(1, samples),
        ray_index.reshape(1, samples),
        expert_index.reshape(1, samples),
        slot_index.reshape(1, samples),
        color_cotangent.reshape(3, 1, color_cotangent.shape[3]),
    )
    whole = pl.BlockSpec(memory_space=pltpu.VMEM)
    out_in, out_w, out_small = pl.pallas_call(
        functools.partial(body, replicas, experts),
        out_shape=(
            jax.ShapeDtypeStruct((samples, width), BF16),
            jax.ShapeDtypeStruct((replicas, layers, piece, width), BF16),
            jax.ShapeDtypeStruct((replicas, (layers + 8) // replicas, width), F32),
        ),
        in_specs=[pl.BlockSpec(memory_space=pltpu.HBM)] * 11,
        out_specs=(whole,) * 3,
        scratch_shapes=[
            *(pltpu.VMEM(a.shape, a.dtype) for a in operands),
            dma((11,)),
            pltpu.VMEM((layers + 1, cells, width), BF16),
            pltpu.VMEM((lanes, width), F32),
            pltpu.VMEM((experts, cap, width), BF16),
            pltpu.VMEM((experts, cap, width), BF16),
            pltpu.VMEM((experts, 1, lanes), F32),
            pltpu.VMEM((experts, 1, lanes), F32),
            pltpu.VMEM((experts, 1, lanes), F32),
            pltpu.VMEM((experts, 1, lanes), F32),
            pltpu.VMEM((experts, cap, width), BF16),
            pltpu.VMEM((experts, cap, width), BF16),
            pltpu.VMEM((layers, replicas, piece, width), F32),
            pltpu.VMEM((2, steps * layers, piece, width), BF16),
            pltpu.VMEM((2, steps, layers, piece, width), BF16),
            pltpu.VMEM((layers, piece, width), BF16),
            pltpu.VMEM((layers, piece, width), BF16),
            pltpu.VMEM((8, width), F32),
            pltpu.VMEM((3, 8, 8, width), F32),
            pltpu.VMEM((replicas, (layers + 8) // replicas, width), F32),
            pltpu.VMEM((replicas, (layers + 8) // replicas, width), F32),
            dma((4,)),
            dma((4,)),
            dma((2,)),
            dma((2, steps, layers)),
            dma((2,)),
            dma((2, layers)),
            dma((2,)),
            dma((2, steps, layers)),
            dma((3,)),
            dma((3,)),
            dma((2,)),
            dma((2,)),
        ],
        compiler_params=pltpu.CompilerParams(
            collective_id=0, has_side_effects=True, vmem_limit_bytes=32 * 1024 * 1024
        ),
    )(*(pltpu.with_memory_space_constraint(a, pltpu.HBM) for a in operands))
    grad_inputs, grad_weights, grad_biases, grad_head_weight, grad_head_bias = pl.pallas_call(
        write_out,
        out_shape=(
            jax.ShapeDtypeStruct((samples, width), BF16),
            jax.ShapeDtypeStruct((layers, replicas, piece, width), F32),
            jax.ShapeDtypeStruct((layers, width), F32),
            jax.ShapeDtypeStruct((4, width), F32),
            jax.ShapeDtypeStruct((1, 4), F32),
        ),
        in_specs=[whole] * 3,
        out_specs=(whole, pl.BlockSpec(memory_space=pl.ANY), whole, whole, whole),
        scratch_shapes=[
            pltpu.VMEM((layers, replicas, piece, width), F32),
            dma((layers,)),
        ],
        compiler_params=pltpu.CompilerParams(vmem_limit_bytes=16 * 1024 * 1024),
    )(out_in, out_w, out_small)
    return (
        grad_inputs.reshape(1, 1, samples, width),
        grad_weights.reshape(1, layers, width, width),
        grad_biases[None],
        grad_head_weight,
        grad_head_bias.reshape(4),
    )


def solution(mesh):
    in_specs = (
        P("dp", "expert", None, None),
        P("expert", None, None, None),
        P("expert", None, None),
        P(),
        P(),
        P("dp", "expert", None),
        P("dp", "expert", None),
        P("dp", "expert", None),
        P("dp", "expert", None),
        P("dp", "expert", None),
        P("dp", "expert", None, None),
    )
    out_specs = (
        P("dp", "expert", None, None),
        P("expert", None, None, None),
        P("expert", None, None),
        P(),
        P(),
    )
    return jax.shard_map(
        functools.partial(per_device, mesh.shape["dp"], mesh.shape["expert"]),
        mesh=mesh,
        in_specs=in_specs,
        out_specs=out_specs,
        check_vma=False,
    )
```
